32 devices in a mesh: span: 16 (over z, y, x), wall: 2 (over core).
Axes of the slice: x: 2, y: 2, z: 4, core: 2. Of those that a mesh axis runs over, the one named last changes fastest.
Arguments:
- velocity: bfloat16 [64, 3, 8, 128, 256], P(None, None, None, 'span', 'wall'), may hold values from -1080 to 1080, as said below
- wall_metric: float32 [256], P('wall'), may hold values from 0.5 to 2
Outputs:
- modes: bfloat16 [64, 3, 2, 128, 256], P(None, None, None, 'span', 'wall')
- r_factor: float32 [64, 64], replicated
The draws below stay inside these ranges and needn't reach their ends.
Inputs may be any that keep to these rules, and one draw needn't show every extreme that they name: velocity fields of order up to a few hundred.
All inputs are finite; a program needn't handle non-finite values.
Results may differ from the reference program's by a relative error of at most 0.0063.
Values may be sent and summed in bfloat16 or wider, within the bound.
A program may use at most 64 MiB of HBM per device.

```python
import math
import jax
import jax.numpy as jnp
from jax import lax

M = 64
XP = 2
NZ = 128
NY = 256
NROW = 196608


def draw_velocity(key, part):
    shape = (M, 3, XP + 6, NZ, NY)
    common_key = jax.random.fold_in(key, 11)
    own_key = jax.random.fold_in(key, 12)
    scale_key = jax.random.fold_in(key, 13)
    rough_key = jax.random.fold_in(key, 14)
    common = jnp.clip(jax.random.normal(common_key, (1, 3, XP + 6, NZ, NY), jnp.float32), -5.0, 5.0)
    own = jnp.clip(jax.random.normal(own_key, shape, jnp.float32), -5.0, 5.0)
    span_rise = 1.0 + 2.0 * jnp.arange(NZ, dtype=jnp.float32) / NZ
    wall_rise = 1.0 + 2.0 * jnp.arange(NY, dtype=jnp.float32) / NY
    scales = jnp.exp(jax.random.uniform(scale_key, (M, 1, 1, 1, 1), jnp.float32, 0.0, 2.302585))
    rough = jax.random.uniform(rough_key, (1, 1, 1, NZ, NY), jnp.float32, 0.6, 1.5)
    envelope = span_rise[:, None] * wall_rise[None, :] * rough
    return (scales * envelope * (0.6 * common + own)).astype(jnp.bfloat16)


def block_levels(rng, shape, split, least, largest):
    level = 1.0
    for position, parts in split:
        heights = jax.random.uniform(jax.random.fold_in(jax.random.fold_in(rng, 6), position), (parts,), jnp.float32, least / len(split), largest / len(split))
        level = level * jnp.repeat(jnp.exp(heights), shape[position] // parts).reshape((-1,) + (1,) * (len(shape) - 1 - position))
    return level


def setup_inputs(seed: int = 0) -> dict:
    key_of = jax.random.split(jax.random.key(seed), 3)
    return {
        "velocity": draw_velocity(jax.random.fold_in(key_of[2], 71), 0),
        "wall_metric": jnp.clip(jnp.exp(math.log(2.0) - 1.3862944 * jax.random.uniform(key_of[1], (NY,), jnp.float32) ** block_levels(key_of[1], (NY,), ((0, 2),), -0.2, 0.2)), 0.5, 2.0),
    }


def stencil(padded, axis, length):

    def take(k):
        return lax.slice_in_dim(padded, 3 + k, 3 + k + length, axis=axis).astype(jnp.float32)
    return (45.0 * (take(1) - take(-1)) - 9.0 * (take(2) - take(-2)) + (take(3) - take(-3))) / 60.0

def factor_lower(gram):
    order = gram.shape[0]
    positions = jnp.arange(order, dtype=jnp.int32)

    def column(index, lower):
        at = jnp.asarray(index).astype(jnp.int32)
        above = lax.dynamic_slice_in_dim(gram, at, 1, 1)[:, 0]
        row_j = lax.dynamic_slice_in_dim(lower, at, 1, 0)[0]
        rest = above - lax.optimization_barrier(jnp.sum(lower * row_j[None, :], axis=1))
        pivot = jnp.sqrt(lax.dynamic_slice_in_dim(rest, at, 1, 0)[0])
        keep = (positions >= at).astype(gram.dtype)
        pick = (positions == at).astype(gram.dtype)
        return lower + (keep * rest / pivot)[:, None] * pick[None, :]
    return lax.fori_loop(0, order, column, jnp.zeros_like(gram))

def invert_lower(lower):
    order = lower.shape[0]
    positions = jnp.arange(order, dtype=jnp.int32)

    def row_step(index, inverse):
        at = jnp.asarray(index).astype(jnp.int32)
        pick = (positions == at).astype(lower.dtype)
        row_l = lax.dynamic_slice_in_dim(lower, at, 1, 0)[0]
        pivot = lax.dynamic_slice_in_dim(row_l, at, 1, 0)[0]
        new_row = (pick - lax.optimization_barrier(jnp.sum(row_l[:, None] * inverse, axis=0))) / pivot
        return inverse + pick[:, None] * new_row[None, :]
    return lax.fori_loop(0, order, row_step, jnp.zeros_like(lower))

def reference(velocity, wall_metric):

    def single(snap):
        inner = snap[:, 3:3 + XP]
        zpad = jnp.concatenate([inner[:, :, -3:, :], inner, inner[:, :, :3, :]], axis=2)
        ypad = jnp.pad(inner, ((0, 0), (0, 0), (0, 0), (3, 3)))
        du_dz = stencil(zpad[0], 1, NZ)
        dv_dz = stencil(zpad[1], 1, NZ)
        du_dy = wall_metric * stencil(ypad[0], 2, NY)
        dw_dy = wall_metric * stencil(ypad[2], 2, NY)
        dv_dx = stencil(snap[1], 0, XP)
        dw_dx = stencil(snap[2], 0, XP)
        return jnp.stack([dw_dy - dv_dz, du_dz - dw_dx, dv_dx - du_dy], axis=0).astype(jnp.bfloat16)
    vorticity = lax.map(single, velocity)
    flat = vorticity.reshape(M, -1)
    gram = jnp.dot(flat, flat.T, preferred_element_type=jnp.float32) / NROW
    lower = factor_lower(gram)
    upper = lower.T
    r_inverse = invert_lower(lower).T.astype(jnp.bfloat16)
    modes = jnp.dot(r_inverse.T, flat, preferred_element_type=jnp.float32).astype(jnp.bfloat16)
    return (modes.reshape(vorticity.shape), upper)
```

```python
import functools

import jax
import jax.numpy as jnp
import ml_dtypes
import numpy as np
from jax import lax
from jax.experimental import pallas as pl
from jax.experimental.pallas import tpu as pltpu
from jax.sharding import PartitionSpec as P

MESH = pl.DeviceIdType.MESH
BF = jnp.bfloat16
F32 = jnp.float32


def coef(offset):
    table = {1: 45.0, 2: -9.0, 3: 1.0}
    size = np.abs(offset)
    out = np.zeros(offset.shape, np.float32)
    for step, value in table.items():
        out = np.where(size == step, value * np.sign(offset), out)
    return out


def constants(snaps, cells, lanes, planes):
    half = snaps // 2
    z = np.arange(cells)
    r = np.arange(3)
    eye = np.eye(half, dtype=np.float32)
    pick = np.concatenate(
        [
            np.kron(eye, (z[None, :] == r[:, None]).astype(np.float32)),
            np.kron(eye, (z[None, :] == cells - 3 + r[:, None]).astype(np.float32)),
        ],
        axis=0,
    )
    inside = np.kron(eye, coef(z[None, :] - z[:, None]))
    outside = np.concatenate(
        [
            np.kron(eye, coef(r[None, :] - 3 - z[:, None])),
            np.kron(eye, coef(cells + r[None, :] - z[:, None])),
        ],
        axis=1,
    )
    y = np.arange(lanes)
    wall = coef(y[:, None] - y[None, :])
    packs = 4 * planes
    step = lanes // packs
    gather = np.zeros((packs, lanes, lanes), np.float32)
    scatter = np.zeros((2, lanes, packs, lanes), np.float32)
    for g in range(packs):
        for t in range(3):
            gather[g, t, g * step + t] = 1.0
            gather[g, lanes - 3 + t, g * step + 3 + t] = 1.0
            scatter[0, g * step + 3 + t, g] = coef(t - 3 - y)
            scatter[1, g * step + t, g] = coef(lanes + t - y)
    gather = gather.reshape(packs * lanes, lanes)
    scatter = scatter.reshape(2 * lanes, packs * lanes)
    owner = np.arange(snaps * cells) // cells
    one = (owner[None, :] == np.arange(snaps)[:, None]).astype(np.float32)
    spread = np.concatenate([np.zeros_like(one), one], axis=0)
    tables = (pick, inside, outside, gather, wall, scatter, spread)
    return [jnp.asarray(a.astype(ml_dtypes.bfloat16)) for a in tables]


def dot(a, b):
    return jnp.dot(a, b, preferred_element_type=F32)


def eliminate(rows):
    groups = list(rows)
    count = len(groups)
    sub = lax.broadcasted_iota(jnp.int32, (8, 128), 0)

    def wide(value):
        return jnp.broadcast_to(value, (8, 128))

    for b in range(count):
        at = 8 * b
        p = [wide(groups[b][k : k + 1, :]) for k in range(8)]
        s = {(k, l): wide(p[k][:, at + l : at + l + 1]) for k in range(8) for l in range(k, 8)}
        inv, f = [], {}
        for k in range(8):
            inv.append(1.0 / s[k, k])
            for l in range(k + 1, 8):
                f[k, l] = s[k, l] * inv[k]
                for m in range(l, 8):
                    s[l, m] = s[l, m] - f[k, l] * s[k, m]
        for k in range(8):
            for l in range(k + 1, 8):
                p[l] = p[l] - f[k, l] * p[k]
        scaled = [p[k] * inv[k] for k in range(8)]
        for i in range(b + 1, count):
            c = [wide(groups[i][:, at + k : at + k + 1]) for k in range(8)]
            value = groups[i]
            for k in range(8):
                for l in range(k + 1, 8):
                    c[l] = c[l] - c[k] * f[k, l]
                value = value - c[k] * scaled[k]
            groups[i] = value
        yield p, [s[k, k] for k in range(8)]


def kernel(
    span_count, wall_count, total_rows,
    vel, metric_hbm, pick_hbm, inside_hbm, outside_hbm, gather_hbm, wall_hbm, scatter_hbm,
    vort_hbm, gram_ref,
    metric_ref, pick_ref, inside_ref, outside_ref, gather_ref, wall_ref, scatter_ref,
    u_buf, v_buf, w_buf, flat, send_buf, halo_buf, ysend_buf, ylo_buf, yhi_buf, acc, vort, vz,
    stage, piece_buf, sum_buf, full_buf,
    local_sem, hs_sem, hr_sem, ys_sem, yr_sem, ps_sem, pr_sem, ss_sem, sr_sem, fs_sem, fr_sem, seen,
):
    snaps, planes = u_buf.shape[0], u_buf.shape[1]
    cells, lanes = vel.shape[3], vel.shape[4]
    half = snaps // 2
    rows = half * cells
    edge = half * 3
    me = lax.axis_index("span")
    mw = lax.axis_index("wall")

    def ring(d):
        return lax.rem(me + span_count + d, span_count)

    down, up = ring(-1), ring(1)

    def load(i, src, dst):
        copy = pltpu.make_async_copy(src, dst, local_sem.at[i])
        copy.start()
        return copy

    mid = pl.ds(3, planes)
    load_pick = load(0, pick_hbm, pick_ref)
    load_u = load(1, vel.at[:, 0, mid], u_buf)
    load_v = load(2, vel.at[:, 1, mid], v_buf.at[:, mid])
    load_rest = [
        load(3, gather_hbm, gather_ref),
        load(4, vel.at[:, 2], w_buf),
        load(5, vel.at[:, 1, pl.ds(0, 3)], v_buf.at[:, pl.ds(0, 3)]),
        load(6, vel.at[:, 1, pl.ds(3 + planes, 3)], v_buf.at[:, pl.ds(3 + planes, 3)]),
        load(7, wall_hbm, wall_ref),
        load(8, scatter_hbm, scatter_ref),
        load(9, metric_hbm, metric_ref),
        load(10, inside_hbm, inside_ref),
        load(11, outside_hbm, outside_ref),
    ]

    barrier = pltpu.get_barrier_semaphore()
    for peer in (down, up):
        pl.semaphore_signal(barrier, inc=1, device_id=(peer, mw), device_id_type=MESH)
    for d in range(1, wall_count):
        pl.semaphore_signal(
            barrier, inc=1, device_id=(me, lax.rem(mw + d, wall_count)), device_id_type=MESH
        )

    def tell(phase):
        for peer in (ring(-(1 << phase)), ring(1 << phase)):
            pl.semaphore_signal(seen.at[phase], inc=1, device_id=(peer, mw), device_id_type=MESH)

    def hear(phase):
        pl.semaphore_wait(seen.at[phase], 2)

    def rows_of(value):
        return value.astype(F32).reshape(rows, lanes).astype(BF)

    def wide(buf, p):
        return jnp.concatenate(
            [rows_of(buf[k * half : (k + 1) * half, p]) for k in range(2)], axis=1
        )

    halo = []
    for c in range(2):
        if c == 0:
            load_pick.wait()
            load_u.wait()
        else:
            load_v.wait()
        for p in range(planes):
            f = wide(u_buf, p) if c == 0 else wide(v_buf, 3 + p)
            flat[c, p] = f
            send_buf[c, p] = dot(pick_ref[...], f).astype(BF)
            if c == 0 and p == 0:
                pl.semaphore_wait(barrier, 2 + wall_count - 1)
            to_down = pltpu.make_async_remote_copy(
                send_buf.at[c, p, pl.ds(0, edge)], halo_buf.at[c, p, pl.ds(edge, edge)],
                hs_sem.at[c, p, 0], hr_sem.at[c, p, 0],
                device_id=(down, mw), device_id_type=MESH,
            )
            to_up = pltpu.make_async_remote_copy(
                send_buf.at[c, p, pl.ds(edge, edge)], halo_buf.at[c, p, pl.ds(0, edge)],
                hs_sem.at[c, p, 1], hr_sem.at[c, p, 1],
                device_id=(up, mw), device_id_type=MESH,
            )
            to_down.start()
            to_up.start()
            halo.append((to_down, to_up))

    phases = seen.shape[0]
    tell(0)
    for copy in load_rest:
        copy.wait()
    for p in range(planes):
        flat[2, p] = wide(w_buf, 3 + p)
    ysend_buf[...] = dot(
        jnp.concatenate([flat[2 * c, p] for c in range(2) for p in range(planes)], axis=1),
        gather_ref[...],
    ).astype(BF)

    y_up = pltpu.make_async_remote_copy(
        ysend_buf, ylo_buf, ys_sem.at[0], yr_sem.at[0],
        device_id=(me, lax.rem(mw + 1, wall_count)), device_id_type=MESH,
    )
    y_down = pltpu.make_async_remote_copy(
        ysend_buf, yhi_buf, ys_sem.at[1], yr_sem.at[1],
        device_id=(me, lax.rem(mw + wall_count - 1, wall_count)), device_id_type=MESH,
    )

    @pl.when(mw < wall_count - 1)
    def _():
        y_up.start()

    @pl.when(mw > 0)
    def _():
        y_down.start()

    @pl.when(mw == 0)
    def _():
        ylo_buf[...] = jnp.zeros_like(ylo_buf)

    @pl.when(mw == wall_count - 1)
    def _():
        yhi_buf[...] = jnp.zeros_like(yhi_buf)

    def along_x(k, carry):
        at = pl.ds(k * 4, 4)
        out = pl.ds(pl.multiple_of(k * 4 * cells, 4 * cells), 4 * cells)
        for c, buf in enumerate((v_buf, w_buf)):
            f = [buf[at, q].astype(F32) for q in range(6 + planes)]
            for p in range(planes):
                d = (
                    45.0 * (f[p + 4] - f[p + 2]) - 9.0 * (f[p + 5] - f[p + 1])
                    + (f[p + 6] - f[p])
                ).reshape(4 * cells, lanes)
                if c == 0:
                    acc[2, p, out] = d
                else:
                    acc[1, p, out] = -d
        return carry

    lax.fori_loop(0, snaps // 4, along_x, 0)

    if phases > 0:
        hear(0)
    if phases > 1:
        tell(1)

    @pl.when(mw > 0)
    def _():
        y_up.wait_recv()

    @pl.when(mw < wall_count - 1)
    def _():
        y_down.wait_recv()

    sides = jnp.concatenate([ylo_buf[...], yhi_buf[...]], axis=1)
    metric = metric_ref[...]
    for c in range(2):
        for p in range(planes):
            for k in range(2):
                g = (c * planes + p) * 2 + k
                at = slice(k * rows, (k + 1) * rows)
                f = flat[2 * c, p, :, k * lanes : (k + 1) * lanes]
                d = dot(f, wall_ref[...])
                d = d + dot(sides, scatter_ref[:, g * lanes : (g + 1) * lanes])
                d = d * metric
                if c == 0:
                    acc[2, p, at] = acc[2, p, at] - d
                else:
                    acc[0, p, at] = d

    def finish(comp, p, k, value):
        slab = comp * planes + p
        at = slice(k * rows, (k + 1) * rows)
        v = (value * (1.0 / 60.0)).astype(BF)
        vort[at, slab * lanes : (slab + 1) * lanes] = v
        vz[slab % 2, at] = v.astype(F32)

    def gram_of(slab):
        a = jnp.concatenate(
            [vz[slab % 2, pl.ds(z, snaps, stride=cells), :].astype(BF) for z in range(cells)],
            axis=1,
        )
        return lax.dot_general(
            a, jnp.concatenate([a, a], axis=0), (((1,), (1,)), ((), ())),
            preferred_element_type=F32,
        )

    for p in range(planes):
        for c in range(2):
            d = dot(inside_ref[...], flat[c, p])
            for k in range(2):
                at = slice(k * rows, (k + 1) * rows)
                part = d[:, k * lanes : (k + 1) * lanes]
                if c == 0:
                    acc[1, p, at] = acc[1, p, at] + part
                else:
                    acc[0, p, at] = acc[0, p, at] - part
    g = None
    for p in range(planes):
        for k in range(2):
            finish(2, p, k, acc[2, p, k * rows : (k + 1) * rows])
        part = gram_of(2 * planes + p)
        g = part if g is None else g + part
    if phases > 1:
        hear(1)
    for phase in range(2, phases):
        tell(phase)
        if phase < phases - 1:
            hear(phase)

    for c in range(2):
        for p in range(planes):
            for copy in halo[c * planes + p]:
                copy.wait_recv()
            d = dot(outside_ref[...], halo_buf[c, p])
            for k in range(2):
                at = slice(k * rows, (k + 1) * rows)
                part = d[:, k * lanes : (k + 1) * lanes]
                if c == 0:
                    finish(1, p, k, acc[1, p, at] + part)
                else:
                    finish(0, p, k, acc[0, p, at] - part)
            g = g + gram_of((1 - c) * planes + p)
    store = pltpu.make_async_copy(vort, vort_hbm, local_sem.at[12])
    store.start()
    if phases > 2:
        hear(phases - 1)

    lane = lax.broadcasted_iota(jnp.int32, (half, 2 * snaps), 1)
    packed = jnp.where(lane < snaps, g[:half], g[half:])
    each = half // wall_count
    copies = []

    def remote(src, dst, send, recv, device):
        copy = pltpu.make_async_remote_copy(
            src, dst, send, recv, device_id=device, device_id_type=MESH
        )
        copy.start()
        return copy

    for w in range(wall_count):
        stage[w] = packed[w * each : (w + 1) * each]
    piece_buf[mw] = stage[mw]
    started = []
    for d in range(1, wall_count):
        w = lax.rem(mw + d, wall_count)
        started.append(
            remote(stage.at[w], piece_buf.at[mw], ps_sem.at[d], pr_sem.at[d], (me, w))
        )
    for copy in started:
        copy.wait_recv()
    copies += started
    total = piece_buf[0]
    for w in range(1, wall_count):
        total = total + piece_buf[w]
    sum_buf[me] = total
    started = []
    for d in range(1, span_count):
        started.append(
            remote(sum_buf.at[me], sum_buf.at[me], ss_sem.at[d], sr_sem.at[d], (ring(d), mw))
        )
    for copy in started:
        copy.wait_recv()
    copies += started
    total = sum_buf[0]
    for i in range(1, span_count):
        total = total + sum_buf[i]
    full_buf[mw] = total / total_rows
    started = []
    for d in range(1, wall_count):
        w = lax.rem(mw + d, wall_count)
        started.append(
            remote(full_buf.at[mw], full_buf.at[mw], fs_sem.at[d], fr_sem.at[d], (me, w))
        )
    for copy in started:
        copy.wait_recv()
    copies += started
    for w in range(wall_count):
        gram_ref[w * each : (w + 1) * each] = full_buf[w]

    for copy in copies:
        copy.wait_send()
    for pair in halo:
        for copy in pair:
            copy.wait_send()

    @pl.when(mw < wall_count - 1)
    def _():
        y_up.wait_send()

    @pl.when(mw > 0)
    def _():
        y_down.wait_send()

    store.wait()


def modes_kernel(vort_hbm, gram_ref, spread_ref, out_hbm, r_ref, vort, out, sem):
    snaps, comps, planes, cells, lanes = out.shape
    half = snaps // 2
    load = pltpu.make_async_copy(vort_hbm, vort, sem.at[0])
    load.start()
    gram = gram_ref[...]
    lane = lax.broadcasted_iota(jnp.int32, (half, 2 * snaps), 1)
    sub = lax.broadcasted_iota(jnp.int32, (half, 2 * snaps), 0)
    top = jnp.where(lane < snaps, gram, (lane - snaps == sub).astype(F32))
    bottom = jnp.where(
        lane < snaps, pltpu.roll(gram, snaps, 1), (lane - snaps - half == sub).astype(F32)
    )
    groups = [top[8 * i : 8 * i + 8] for i in range(half // 8)]
    groups += [bottom[8 * i : 8 * i + 8] for i in range(half // 8)]
    lane8 = lax.broadcasted_iota(jnp.int32, (8, 2 * snaps), 1)
    sub8 = lax.broadcasted_iota(jnp.int32, (8, 2 * snaps), 0)
    count = 2
    block = 8 * count
    wide = block * cells
    row_z = lax.rem(lax.broadcasted_iota(jnp.int32, (wide, snaps * cells), 0), cells)
    col_z = lax.rem(lax.broadcasted_iota(jnp.int32, (wide, snaps * cells), 1), cells)
    same = row_z == col_z
    scaled = []
    stores = []
    for b, (p, s) in enumerate(eliminate(groups)):
        q = [p[k] / jnp.sqrt(s[k]) for k in range(8)]
        row = q[0]
        for k in range(1, 8):
            row = jnp.where(sub8 == k, q[k], row)
        row = jnp.where(lane8 < sub8 + 8 * b, 0.0, row)
        r_ref[8 * b : 8 * b + 8] = row[:, :snaps]
        scaled += q
        if b % count == count - 1:
            x = jnp.concatenate(scaled, axis=0).astype(BF)
            scaled = []
            n = b // count
            depth = (n + 1) * wide
            w = dot(x, spread_ref[:, :depth])
            w = jnp.where(same[:, :depth], w, 0.0).astype(BF)
            if n == 0:
                load.wait()
            m = dot(w, vort[:depth])
            at = pl.ds(n * block, block)
            for comp in range(comps):
                for p_ in range(planes):
                    slab = comp * planes + p_
                    out[n * block : (n + 1) * block, comp, p_] = (
                        m[:, slab * lanes : (slab + 1) * lanes]
                        .reshape(block, cells, lanes).astype(BF)
                    )
            store = pltpu.make_async_copy(out.at[at], out_hbm.at[at], sem.at[1 + n])
            store.start()
            stores.append(store)
    for store in stores:
        store.wait()


def per_device(velocity, wall_metric):
    snaps, comps, depth, cells, lanes = velocity.shape
    planes = depth - 6
    spans, walls = lax.axis_size("span"), lax.axis_size("wall")
    phases, reach = 0, 1
    while 2 * reach < spans:
        phases, reach = phases + 1, 2 * reach
    total_rows = 3 * planes * cells * spans * lanes * walls
    *consts, spread = constants(snaps, cells, lanes, planes)
    vmem = pl.BlockSpec(memory_space=pltpu.VMEM)
    hbm = pl.BlockSpec(memory_space=pl.ANY)
    dma = pltpu.SemaphoreType.DMA
    half = snaps // 2
    each = half // walls
    wide = snaps * cells
    rows = half * cells
    edge = half * 3
    slabs = comps * planes
    vorticity, gram = pl.pallas_call(
        functools.partial(kernel, spans, walls, total_rows),
        out_shape=(
            jax.ShapeDtypeStruct((wide, slabs * lanes), BF),
            jax.ShapeDtypeStruct((half, 2 * snaps), F32),
        ),
        in_specs=[hbm] * (2 + len(consts)),
        out_specs=(hbm, vmem),
        scratch_shapes=[
            pltpu.VMEM((1, lanes), F32),
            *[pltpu.VMEM(a.shape, a.dtype) for a in consts],
            pltpu.VMEM((snaps, planes, cells, lanes), BF),
            pltpu.VMEM((snaps, depth, cells, lanes), BF),
            pltpu.VMEM((snaps, depth, cells, lanes), BF),
            pltpu.VMEM((3, planes, rows, 2 * lanes), BF),
            pltpu.VMEM((2, planes, 2 * edge, 2 * lanes), BF),
            pltpu.VMEM((2, planes, 2 * edge, 2 * lanes), BF),
            pltpu.VMEM((rows, lanes), BF),
            pltpu.VMEM((rows, lanes), BF),
            pltpu.VMEM((rows, lanes), BF),
            pltpu.VMEM((3, planes, wide, lanes), F32),
            pltpu.VMEM((wide, slabs * lanes), BF),
            pltpu.VMEM((2, wide, lanes), F32),
            pltpu.VMEM((walls, each, 2 * snaps), F32),
            pltpu.VMEM((walls, each, 2 * snaps), F32),
            pltpu.VMEM((spans, each, 2 * snaps), F32),
            pltpu.VMEM((walls, each, 2 * snaps), F32),
            dma((13,)),
            dma((2, planes, 2)),
            dma((2, planes, 2)),
            dma((2,)),
            dma((2,)),
            dma((walls,)),
            dma((walls,)),
            dma((spans,)),
            dma((spans,)),
            dma((walls,)),
            dma((walls,)),
            pltpu.SemaphoreType.REGULAR((phases,)),
        ],
        compiler_params=pltpu.CompilerParams(
            collective_id=0, has_side_effects=True, vmem_limit_bytes=48 << 20
        ),
        name="pod",
    )(velocity, wall_metric.reshape(1, lanes), *consts)
    return pl.pallas_call(
        modes_kernel,
        out_shape=(
            jax.ShapeDtypeStruct((snaps, comps, planes, cells, lanes), BF),
            jax.ShapeDtypeStruct((snaps, snaps), F32),
        ),
        in_specs=[hbm, vmem, vmem],
        out_specs=(hbm, vmem),
        scratch_shapes=[
            pltpu.VMEM((wide, slabs * lanes), BF),
            pltpu.VMEM((snaps, comps, planes, cells, lanes), BF),
            dma((5,)),
        ],
        name="modes",
    )(vorticity, gram, spread)


def solution(mesh):
    in_specs = (P(None, None, None, "span", "wall"), P("wall"))
    out_specs = (P(None, None, None, "span", "wall"), P())
    return jax.shard_map(
        per_device, mesh=mesh, in_specs=in_specs, out_specs=out_specs, check_vma=False
    )
```

```python
import functools

import jax
import jax.numpy as jnp
import ml_dtypes
import numpy as np
from jax import lax
from jax.experimental import pallas as pl
from jax.experimental.pallas import tpu as pltpu
from jax.sharding import PartitionSpec as P

MESH = pl.DeviceIdType.MESH
BF = jnp.bfloat16
F32 = jnp.float32


def coef(offset):
    table = {1: 45.0, 2: -9.0, 3: 1.0}
    size = np.abs(offset)
    out = np.zeros(offset.shape, np.float32)
    for step, value in table.items():
        out = np.where(size == step, value * np.sign(offset), out)
    return out


def constants(snaps, cells, lanes, planes):
    half = snaps // 2
    z = np.arange(cells)
    r = np.arange(3)
    eye = np.eye(half, dtype=np.float32)
    pick = np.concatenate(
        [
            np.kron(eye, (z[None, :] == r[:, None]).astype(np.float32)),
            np.kron(eye, (z[None, :] == cells - 3 + r[:, None]).astype(np.float32)),
        ],
        axis=0,
    )
    inside = np.kron(eye, coef(z[None, :] - z[:, None]))
    outside = np.concatenate(
        [
            np.kron(eye, coef(r[None, :] - 3 - z[:, None])),
            np.kron(eye, coef(cells + r[None, :] - z[:, None])),
        ],
        axis=1,
    )
    y = np.arange(lanes)
    wall = coef(y[:, None] - y[None, :])
    packs = 4 * planes
    step = lanes // packs
    gather = np.zeros((packs, lanes, lanes), np.float32)
    scatter = np.zeros((2, lanes, packs, lanes), np.float32)
    for g in range(packs):
        for t in range(3):
            gather[g, t, g * step + t] = 1.0
            gather[g, lanes - 3 + t, g * step + 3 + t] = 1.0
            scatter[0, g * step + 3 + t, g] = coef(t - 3 - y)
            scatter[1, g * step + t, g] = coef(lanes + t - y)
    gather = gather.reshape(packs * lanes, lanes)
    scatter = scatter.reshape(2 * lanes, packs * lanes)
    owner = np.arange(snaps * cells) // cells
    one = (owner[None, :] == np.arange(snaps)[:, None]).astype(np.float32)
    spread = np.concatenate([np.zeros_like(one), one], axis=0)
    tables = (pick, inside, outside, gather, wall, scatter, spread)
    return [jnp.asarray(a.astype(ml_dtypes.bfloat16)) for a in tables]


def dot(a, b):
    return jnp.dot(a, b, preferred_element_type=F32)


def eliminate(rows):
    groups = list(rows)
    count = len(groups)
    sub = lax.broadcasted_iota(jnp.int32, (8, 128), 0)

    def wide(value):
        return jnp.broadcast_to(value, (8, 128))

    for b in range(count):
        at = 8 * b
        p = [wide(groups[b][k : k + 1, :]) for k in range(8)]
        s = {(k, l): wide(p[k][:, at + l : at + l + 1]) for k in range(8) for l in range(k, 8)}
        inv, f = [], {}
        for k in range(8):
            inv.append(1.0 / s[k, k])
            for l in range(k + 1, 8):
                f[k, l] = s[k, l] * inv[k]
                for m in range(l, 8):
                    s[l, m] = s[l, m] - f[k, l] * s[k, m]
        for k in range(8):
            for l in range(k + 1, 8):
                p[l] = p[l] - f[k, l] * p[k]
        scaled = [p[k] * inv[k] for k in range(8)]
        for i in range(b + 1, count):
            c = [wide(groups[i][:, at + k : at + k + 1]) for k in range(8)]
            value = groups[i]
            for k in range(8):
                for l in range(k + 1, 8):
                    c[l] = c[l] - c[k] * f[k, l]
                value = value - c[k] * scaled[k]
            groups[i] = value
        yield p, [s[k, k] for k in range(8)]


def kernel(
    span_count, wall_count, total_rows,
    vel, metric_hbm, pick_hbm, inside_hbm, outside_hbm, gather_hbm, wall_hbm, scatter_hbm,
    vort_hbm, gram_ref,
    metric_ref, pick_ref, inside_ref, outside_ref, gather_ref, wall_ref, scatter_ref,
    u_buf, v_buf, w_buf, flat, send_buf, halo_buf, ysend_buf, ylo_buf, yhi_buf, acc, vort, vz,
    stage, piece_buf, sum_buf, full_buf,
    local_sem, hs_sem, hr_sem, ys_sem, yr_sem, ps_sem, pr_sem, ss_sem, sr_sem, fs_sem, fr_sem, seen,
):
    snaps, planes = u_buf.shape[0], u_buf.shape[1]
    cells, lanes = vel.shape[3], vel.shape[4]
    half = snaps // 2
    rows = half * cells
    edge = half * 3
    me = lax.axis_index("span")
    mw = lax.axis_index("wall")

    def ring(d):
        return lax.rem(me + span_count + d, span_count)

    down, up = ring(-1), ring(1)

    def load(i, src, dst):
        copy = pltpu.make_async_copy(src, dst, local_sem.at[i])
        copy.start()
        return copy

    mid = pl.ds(3, planes)
    load_pick = load(0, pick_hbm, pick_ref)
    load_u = load(1, vel.at[:, 0, mid], u_buf)
    load_v = load(2, vel.at[:, 1, mid], v_buf.at[:, mid])
    load_rest = [
        load(3, gather_hbm, gather_ref),
        load(4, vel.at[:, 2], w_buf),
        load(5, vel.at[:, 1, pl.ds(0, 3)], v_buf.at[:, pl.ds(0, 3)]),
        load(6, vel.at[:, 1, pl.ds(3 + planes, 3)], v_buf.at[:, pl.ds(3 + planes, 3)]),
        load(7, wall_hbm, wall_ref),
        load(8, scatter_hbm, scatter_ref),
        load(9, metric_hbm, metric_ref),
        load(10, inside_hbm, inside_ref),
        load(11, outside_hbm, outside_ref),
    ]

    barrier = pltpu.get_barrier_semaphore()
    for peer in (down, up):
        pl.semaphore_signal(barrier, inc=1, device_id=(peer, mw), device_id_type=MESH)
    for d in range(1, wall_count):
        pl.semaphore_signal(
            barrier, inc=1, device_id=(me, lax.rem(mw + d, wall_count)), device_id_type=MESH
        )

    def tell(phase):
        for peer in (ring(-(1 << phase)), ring(1 << phase)):
            pl.semaphore_signal(seen.at[phase], inc=1, device_id=(peer, mw), device_id_type=MESH)

    def hear(phase):
        pl.semaphore_wait(seen.at[phase], 2)

    def rows_of(value):
        return value.astype(F32).reshape(rows, lanes).astype(BF)

    def wide(buf, p):
        return jnp.concatenate(
            [rows_of(buf[k * half : (k + 1) * half, p]) for k in range(2)], axis=1
        )

    halo = []
    for c in range(2):
        if c == 0:
            load_pick.wait()
            load_u.wait()
        else:
            load_v.wait()
        for p in range(planes):
            f = wide(u_buf, p) if c == 0 else wide(v_buf, 3 + p)
            flat[c, p] = f
            send_buf[c, p] = dot(pick_ref[...], f).astype(BF)
            if c == 0 and p == 0:
                pl.semaphore_wait(barrier, 2 + wall_count - 1)
            to_down = pltpu.make_async_remote_copy(
                send_buf.at[c, p, pl.ds(0, edge)], halo_buf.at[c, p, pl.ds(edge, edge)],
                hs_sem.at[c, p, 0], hr_sem.at[c, p, 0],
                device_id=(down, mw), device_id_type=MESH,
            )
            to_up = pltpu.make_async_remote_copy(
                send_buf.at[c, p, pl.ds(edge, edge)], halo_buf.at[c, p, pl.ds(0, edge)],
                hs_sem.at[c, p, 1], hr_sem.at[c, p, 1],
                device_id=(up, mw), device_id_type=MESH,
            )
            to_down.start()
            to_up.start()
            halo.append((to_down, to_up))

    phases = seen.shape[0]
    tell(0)
    for copy in load_rest:
        copy.wait()
    for p in range(planes):
        flat[2, p] = wide(w_buf, 3 + p)
    ysend_buf[...] = dot(
        jnp.concatenate([flat[2 * c, p] for c in range(2) for p in range(planes)], axis=1),
        gather_ref[...],
    ).astype(BF)

    y_up = pltpu.make_async_remote_copy(
        ysend_buf, ylo_buf, ys_sem.at[0], yr_sem.at[0],
        device_id=(me, lax.rem(mw + 1, wall_count)), device_id_type=MESH,
    )
    y_down = pltpu.make_async_remote_copy(
        ysend_buf, yhi_buf, ys_sem.at[1], yr_sem.at[1],
        device_id=(me, lax.rem(mw + wall_count - 1, wall_count)), device_id_type=MESH,
    )

    @pl.when(mw < wall_count - 1)
    def _():
        y_up.start()

    @pl.when(mw > 0)
    def _():
        y_down.start()

    @pl.when(mw == 0)
    def _():
        ylo_buf[...] = jnp.zeros_like(ylo_buf)

    @pl.when(mw == wall_count - 1)
    def _():
        yhi_buf[...] = jnp.zeros_like(yhi_buf)

    def along_x(k, carry):
        at = pl.ds(k * 4, 4)
        out = pl.ds(pl.multiple_of(k * 4 * cells, 4 * cells), 4 * cells)
        for c, buf in enumerate((v_buf, w_buf)):
            f = [buf[at, q].astype(F32) for q in range(6 + planes)]
            for p in range(planes):
                d = (
                    45.0 * (f[p + 4] - f[p + 2]) - 9.0 * (f[p + 5] - f[p + 1])
                    + (f[p + 6] - f[p])
                ).reshape(4 * cells, lanes)
                if c == 0:
                    acc[2, p, out] = d
                else:
                    acc[1, p, out] = -d
        return carry

    lax.fori_loop(0, snaps // 4, along_x, 0)

    if phases > 0:
        hear(0)
    if phases > 1:
        tell(1)

    @pl.when(mw > 0)
    def _():
        y_up.wait_recv()

    @pl.when(mw < wall_count - 1)
    def _():
        y_down.wait_recv()

    sides = jnp.concatenate([ylo_buf[...], yhi_buf[...]], axis=1)
    metric = metric_ref[...]
    for c in range(2):
        for p in range(planes):
            for k in range(2):
                g = (c * planes + p) * 2 + k
                at = slice(k * rows, (k + 1) * rows)
                f = flat[2 * c, p, :, k * lanes : (k + 1) * lanes]
                d = dot(f, wall_ref[...])
                d = d + dot(sides, scatter_ref[:, g * lanes : (g + 1) * lanes])
                d = d * metric
                if c == 0:
                    acc[2, p, at] = acc[2, p, at] - d
                else:
                    acc[0, p, at] = d

    def finish(comp, p, k, value):
        slab = comp * planes + p
        at = slice(k * rows, (k + 1) * rows)
        v = (value * (1.0 / 60.0)).astype(BF)
        vort[at, slab * lanes : (slab + 1) * lanes] = v
        vz[slab % 2, at] = v.astype(F32)

    def gram_of(slab):
        a = jnp.concatenate(
            [vz[slab % 2, pl.ds(z, snaps, stride=cells), :].astype(BF) for z in range(cells)],
            axis=1,
        )
        return lax.dot_general(
            a, jnp.concatenate([a, a], axis=0), (((1,), (1,)), ((), ())),
            preferred_element_type=F32,
        )

    for p in range(planes):
        for c in range(2):
            d = dot(inside_ref[...], flat[c, p])
            for k in range(2):
                at = slice(k * rows, (k + 1) * rows)
                part = d[:, k * lanes : (k + 1) * lanes]
                if c == 0:
                    acc[1, p, at] = acc[1, p, at] + part
                else:
                    acc[0, p, at] = acc[0, p, at] - part
    g = None
    for p in range(planes):
        for k in range(2):
            finish(2, p, k, acc[2, p, k * rows : (k + 1) * rows])
        part = gram_of(2 * planes + p)
        g = part if g is None else g + part
    if phases > 1:
        hear(1)
    for phase in range(2, phases):
        tell(phase)
        if phase < phases - 1:
            hear(phase)

    for c in range(2):
        for p in range(planes):
            for copy in halo[c * planes + p]:
                copy.wait_recv()
            d = dot(outside_ref[...], halo_buf[c, p])
            for k in range(2):
                at = slice(k * rows, (k + 1) * rows)
                part = d[:, k * lanes : (k + 1) * lanes]
                if c == 0:
                    finish(1, p, k, acc[1, p, at] + part)
                else:
                    finish(0, p, k, acc[0, p, at] - part)
            g = g + gram_of((1 - c) * planes + p)
    store = pltpu.make_async_copy(vort, vort_hbm, local_sem.at[12])
    store.start()
    if phases > 2:
        hear(phases - 1)

    lane = lax.broadcasted_iota(jnp.int32, (half, 2 * snaps), 1)
    packed = jnp.where(lane < snaps, g[:half], g[half:])
    each = half // wall_count
    copies = []

    def remote(src, dst, send, recv, device):
        copy = pltpu.make_async_remote_copy(
            src, dst, send, recv, device_id=device, device_id_type=MESH
        )
        copy.start()
        return copy

    for w in range(wall_count):
        stage[w] = packed[w * each : (w + 1) * each]
    piece_buf[mw] = stage[mw]
    started = []
    for d in range(1, wall_count):
        w = lax.rem(mw + d, wall_count)
        started.append(
            remote(stage.at[w], piece_buf.at[mw], ps_sem.at[d], pr_sem.at[d], (me, w))
        )
    for copy in started:
        copy.wait_recv()
    copies += started
    total = piece_buf[0]
    for w in range(1, wall_count):
        total = total + piece_buf[w]
    sum_buf[me] = total
    started = []
    for d in range(1, span_count):
        started.append(
            remote(sum_buf.at[me], sum_buf.at[me], ss_sem.at[d], sr_sem.at[d], (ring(d), mw))
        )
    for copy in started:
        copy.wait_recv()
    copies += started
    total = sum_buf[0]
    for i in range(1, span_count):
        total = total + sum_buf[i]
    full_buf[mw] = total / total_rows
    started = []
    for d in range(1, wall_count):
        w = lax.rem(mw + d, wall_count)
        started.append(
            remote(full_buf.at[mw], full_buf.at[mw], fs_sem.at[d], fr_sem.at[d], (me, w))
        )
    for copy in started:
        copy.wait_recv()
    copies += started
    for w in range(wall_count):
        gram_ref[w * each : (w + 1) * each] = full_buf[w]

    for copy in copies:
        copy.wait_send()
    for pair in halo:
        for copy in pair:
            copy.wait_send()

    @pl.when(mw < wall_count - 1)
    def _():
        y_up.wait_send()

    @pl.when(mw > 0)
    def _():
        y_down.wait_send()

    store.wait()


def modes_kernel(vort_hbm, gram_ref, spread_ref, out_hbm, r_ref, vort, out, sem):
    snaps, comps, planes, cells, lanes = out.shape
    half = snaps // 2
    load = pltpu.make_async_copy(vort_hbm, vort, sem.at[0])
    load.start()
    gram = gram_ref[...]
    lane = lax.broadcasted_iota(jnp.int32, (half, 2 * snaps), 1)
    sub = lax.broadcasted_iota(jnp.int32, (half, 2 * snaps), 0)
    top = jnp.where(lane < snaps, gram, (lane - snaps == sub).astype(F32))
    bottom = jnp.where(
        lane < snaps, pltpu.roll(gram, snaps, 1), (lane - snaps - half == sub).astype(F32)
    )
    groups = [top[8 * i : 8 * i + 8] for i in range(half // 8)]
    groups += [bottom[8 * i : 8 * i + 8] for i in range(half // 8)]
    lane8 = lax.broadcasted_iota(jnp.int32, (8, 2 * snaps), 1)
    sub8 = lax.broadcasted_iota(jnp.int32, (8, 2 * snaps), 0)
    count = 2
    block = 8 * count
    wide = block * cells
    row_z = lax.rem(lax.broadcasted_iota(jnp.int32, (wide, snaps * cells), 0), cells)
    col_z = lax.rem(lax.broadcasted_iota(jnp.int32, (wide, snaps * cells), 1), cells)
    same = row_z == col_z
    scaled = []
    stores = []
    for b, (p, s) in enumerate(eliminate(groups)):
        q = [p[k] / jnp.sqrt(s[k]) for k in range(8)]
        row = q[0]
        for k in range(1, 8):
            row = jnp.where(sub8 == k, q[k], row)
        row = jnp.where(lane8 < sub8 + 8 * b, 0.0, row)
        r_ref[8 * b : 8 * b + 8] = row[:, :snaps]
        scaled += q
        if b % count == count - 1:
            x = jnp.concatenate(scaled, axis=0).astype(BF)
            scaled = []
            n = b // count
            depth = (n + 1) * wide
            w = dot(x, spread_ref[:, :depth])
            w = jnp.where(same[:, :depth], w, 0.0).astype(BF)
            if n == 0:
                load.wait()
            m = dot(w, vort[:depth])
            at = pl.ds(n * block, block)
            for comp in range(comps):
                for p_ in range(planes):
                    slab = comp * planes + p_
                    out[n * block : (n + 1) * block, comp, p_] = (
                        m[:, slab * lanes : (slab + 1) * lanes]
                        .reshape(block, cells, lanes).astype(BF)
                    )
            store = pltpu.make_async_copy(out.at[at], out_hbm.at[at], sem.at[1 + n])
            store.start()
            stores.append(store)
    for store in stores:
        store.wait()


def per_device(velocity, wall_metric):
    snaps, comps, depth, cells, lanes = velocity.shape
    planes = depth - 6
    spans, walls = lax.axis_size("span"), lax.axis_size("wall")
    phases, reach = 0, 1
    while 2 * reach < spans:
        phases, reach = phases + 1, 2 * reach
    total_rows = 3 * planes * cells * spans * lanes * walls
    *consts, spread = constants(snaps, cells, lanes, planes)
    vmem = pl.BlockSpec(memory_space=pltpu.VMEM)
    hbm = pl.BlockSpec(memory_space=pl.ANY)
    dma = pltpu.SemaphoreType.DMA
    half = snaps // 2
    each = half // walls
    wide = snaps * cells
    rows = half * cells
    edge = half * 3
    slabs = comps * planes
    vorticity, gram = pl.pallas_call(
        functools.partial(kernel, spans, walls, total_rows),
        out_shape=(
            jax.ShapeDtypeStruct((wide, slabs * lanes), BF),
            jax.ShapeDtypeStruct((half, 2 * snaps), F32),
        ),
        in_specs=[hbm] * (2 + len(consts)),
        out_specs=(hbm, vmem),
        scratch_shapes=[
            pltpu.VMEM((1, lanes), F32),
            *[pltpu.VMEM(a.shape, a.dtype) for a in consts],
            pltpu.VMEM((snaps, planes, cells, lanes), BF),
            pltpu.VMEM((snaps, depth, cells, lanes), BF),
            pltpu.VMEM((snaps, depth, cells, lanes), BF),
            pltpu.VMEM((3, planes, rows, 2 * lanes), BF),
            pltpu.VMEM((2, planes, 2 * edge, 2 * lanes), BF),
            pltpu.VMEM((2, planes, 2 * edge, 2 * lanes), BF),
            pltpu.VMEM((rows, lanes), BF),
            pltpu.VMEM((rows, lanes), BF),
            pltpu.VMEM((rows, lanes), BF),
            pltpu.VMEM((3, planes, wide, lanes), F32),
            pltpu.VMEM((wide, slabs * lanes), BF),
            pltpu.VMEM((2, wide, lanes), F32),
            pltpu.VMEM((walls, each, 2 * snaps), F32),
            pltpu.VMEM((walls, each, 2 * snaps), F32),
            pltpu.VMEM((spans, each, 2 * snaps), F32),
            pltpu.VMEM((walls, each, 2 * snaps), F32),
            dma((13,)),
            dma((2, planes, 2)),
            dma((2, planes, 2)),
            dma((2,)),
            dma((2,)),
            dma((walls,)),
            dma((walls,)),
            dma((spans,)),
            dma((spans,)),
            dma((walls,)),
            dma((walls,)),
            pltpu.SemaphoreType.REGULAR((phases,)),
        ],
        compiler_params=pltpu.CompilerParams(
            collective_id=0, has_side_effects=True, vmem_limit_bytes=60 << 20
        ),
        name="pod",
    )(velocity, wall_metric.reshape(1, lanes), *consts)
    return pl.pallas_call(
        modes_kernel,
        out_shape=(
            jax.ShapeDtypeStruct((snaps, comps, planes, cells, lanes), BF),
            jax.ShapeDtypeStruct((snaps, snaps), F32),
        ),
        in_specs=[hbm, vmem, vmem],
        out_specs=(hbm, vmem),
        scratch_shapes=[
            pltpu.VMEM((wide, slabs * lanes), BF),
            pltpu.VMEM((snaps, comps, planes, cells, lanes), BF),
            dma((5,)),
        ],
        compiler_params=pltpu.CompilerParams(vmem_limit_bytes=60 << 20),
        name="modes",
    )(vorticity, gram, spread)


def solution(mesh):
    in_specs = (P(None, None, None, "span", "wall"), P("wall"))
    out_specs = (P(None, None, None, "span", "wall"), P())
    return jax.shard_map(
        per_device, mesh=mesh, in_specs=in_specs, out_specs=out_specs, check_vma=False
    )
```

```python
import functools

import jax
import jax.numpy as jnp
import ml_dtypes
import numpy as np
from jax import lax
from jax.experimental import pallas as pl
from jax.experimental.pallas import tpu as pltpu
from jax.sharding import PartitionSpec as P

MESH = pl.DeviceIdType.MESH
BF = jnp.bfloat16
F32 = jnp.float32


def coef(offset):
    table = {1: 45.0, 2: -9.0, 3: 1.0}
    size = np.abs(offset)
    out = np.zeros(offset.shape, np.float32)
    for step, value in table.items():
        out = np.where(size == step, value * np.sign(offset), out)
    return out


def constants(snaps, cells, lanes, planes):
    half = snaps // 2
    z = np.arange(cells)
    r = np.arange(3)
    eye = np.eye(half, dtype=np.float32)
    pick = np.concatenate(
        [
            np.kron(eye, (z[None, :] == r[:, None]).astype(np.float32)),
            np.kron(eye, (z[None, :] == cells - 3 + r[:, None]).astype(np.float32)),
        ],
        axis=0,
    )
    inside = np.kron(eye, coef(z[None, :] - z[:, None]))
    outside = np.concatenate(
        [
            np.kron(eye, coef(r[None, :] - 3 - z[:, None])),
            np.kron(eye, coef(cells + r[None, :] - z[:, None])),
        ],
        axis=1,
    )
    y = np.arange(lanes)
    wall = coef(y[:, None] - y[None, :])
    packs = 4 * planes
    step = lanes // packs
    gather = np.zeros((packs, lanes, lanes), np.float32)
    scatter = np.zeros((2, lanes, packs, lanes), np.float32)
    for g in range(packs):
        for t in range(3):
            gather[g, t, g * step + t] = 1.0
            gather[g, lanes - 3 + t, g * step + 3 + t] = 1.0
            scatter[0, g * step + 3 + t, g] = coef(t - 3 - y)
            scatter[1, g * step + t, g] = coef(lanes + t - y)
    gather = gather.reshape(packs * lanes, lanes)
    scatter = scatter.reshape(2 * lanes, packs * lanes)
    owner = np.arange(snaps * cells) // cells
    one = (owner[None, :] == np.arange(snaps)[:, None]).astype(np.float32)
    spread = np.concatenate([np.zeros_like(one), one], axis=0)
    tables = (pick, inside, outside, gather, wall, scatter, spread)
    return [jnp.asarray(a.astype(ml_dtypes.bfloat16)) for a in tables]


def dot(a, b):
    return jnp.dot(a, b, preferred_element_type=F32)


def eliminate(rows):
    groups = list(rows)
    count = len(groups)
    sub = lax.broadcasted_iota(jnp.int32, (8, 128), 0)

    def wide(value):
        return jnp.broadcast_to(value, (8, 128))

    for b in range(count):
        at = 8 * b
        p = [wide(groups[b][k : k + 1, :]) for k in range(8)]
        s = {(k, l): wide(p[k][:, at + l : at + l + 1]) for k in range(8) for l in range(k, 8)}
        inv, f = [], {}
        for k in range(8):
            inv.append(1.0 / s[k, k])
            for l in range(k + 1, 8):
                f[k, l] = s[k, l] * inv[k]
                for m in range(l, 8):
                    s[l, m] = s[l, m] - f[k, l] * s[k, m]
        for k in range(8):
            for l in range(k + 1, 8):
                p[l] = p[l] - f[k, l] * p[k]
        scaled = [p[k] * inv[k] for k in range(8)]
        for i in range(b + 1, count):
            c = [wide(groups[i][:, at + k : at + k + 1]) for k in range(8)]
            value = groups[i]
            for k in range(8):
                for l in range(k + 1, 8):
                    c[l] = c[l] - c[k] * f[k, l]
                value = value - c[k] * scaled[k]
            groups[i] = value
        yield p, [s[k, k] for k in range(8)]


def kernel(
    span_count, wall_count, total_rows,
    vel, metric_hbm, pick_hbm, inside_hbm, outside_hbm, gather_hbm, wall_hbm, scatter_hbm,
    vort, gram_ref,
    metric_ref, pick_ref, inside_ref, outside_ref, gather_ref, wall_ref, scatter_ref,
    u_buf, v_buf, w_buf, flat, send_buf, halo_buf, ysend_buf, ylo_buf, yhi_buf, acc, vz,
    stage, piece_buf, sum_buf, full_buf,
    local_sem, hs_sem, hr_sem, ys_sem, yr_sem, ps_sem, pr_sem, ss_sem, sr_sem, fs_sem, fr_sem, seen,
):
    snaps, planes = u_buf.shape[0], u_buf.shape[1]
    cells, lanes = vel.shape[3], vel.shape[4]
    half = snaps // 2
    rows = half * cells
    edge = half * 3
    me = lax.axis_index("span")
    mw = lax.axis_index("wall")

    def ring(d):
        return lax.rem(me + span_count + d, span_count)

    down, up = ring(-1), ring(1)

    def load(i, src, dst):
        copy = pltpu.make_async_copy(src, dst, local_sem.at[i])
        copy.start()
        return copy

    mid = pl.ds(3, planes)
    load_pick = load(0, pick_hbm, pick_ref)
    load_u = load(1, vel.at[:, 0, mid], u_buf)
    load_v = load(2, vel.at[:, 1, mid], v_buf.at[:, mid])
    load_rest = [
        load(3, gather_hbm, gather_ref),
        load(4, vel.at[:, 2], w_buf),
        load(5, vel.at[:, 1, pl.ds(0, 3)], v_buf.at[:, pl.ds(0, 3)]),
        load(6, vel.at[:, 1, pl.ds(3 + planes, 3)], v_buf.at[:, pl.ds(3 + planes, 3)]),
        load(7, wall_hbm, wall_ref),
        load(8, scatter_hbm, scatter_ref),
        load(9, metric_hbm, metric_ref),
        load(10, inside_hbm, inside_ref),
        load(11, outside_hbm, outside_ref),
    ]

    barrier = pltpu.get_barrier_semaphore()
    for peer in (down, up):
        pl.semaphore_signal(barrier, inc=1, device_id=(peer, mw), device_id_type=MESH)
    for d in range(1, wall_count):
        pl.semaphore_signal(
            barrier, inc=1, device_id=(me, lax.rem(mw + d, wall_count)), device_id_type=MESH
        )

    def tell(phase):
        for peer in (ring(-(1 << phase)), ring(1 << phase)):
            pl.semaphore_signal(seen.at[phase], inc=1, device_id=(peer, mw), device_id_type=MESH)

    def hear(phase):
        pl.semaphore_wait(seen.at[phase], 2)

    def rows_of(value):
        return value.astype(F32).reshape(rows, lanes).astype(BF)

    def wide(buf, p):
        return jnp.concatenate(
            [rows_of(buf[k * half : (k + 1) * half, p]) for k in range(2)], axis=1
        )

    halo = []
    for c in range(2):
        if c == 0:
            load_pick.wait()
            load_u.wait()
        else:
            load_v.wait()
        for p in range(planes):
            f = wide(u_buf, p) if c == 0 else wide(v_buf, 3 + p)
            flat[c, p] = f
            send_buf[c, p] = dot(pick_ref[...], f).astype(BF)
            if c == 0 and p == 0:
                pl.semaphore_wait(barrier, 2 + wall_count - 1)
            to_down = pltpu.make_async_remote_copy(
                send_buf.at[c, p, pl.ds(0, edge)], halo_buf.at[c, p, pl.ds(edge, edge)],
                hs_sem.at[c, p, 0], hr_sem.at[c, p, 0],
                device_id=(down, mw), device_id_type=MESH,
            )
            to_up = pltpu.make_async_remote_copy(
                send_buf.at[c, p, pl.ds(edge, edge)], halo_buf.at[c, p, pl.ds(0, edge)],
                hs_sem.at[c, p, 1], hr_sem.at[c, p, 1],
                device_id=(up, mw), device_id_type=MESH,
            )
            to_down.start()
            to_up.start()
            halo.append((to_down, to_up))

    phases = seen.shape[0]
    tell(0)
    for copy in load_rest:
        copy.wait()
    for p in range(planes):
        flat[2, p] = wide(w_buf, 3 + p)
    ysend_buf[...] = dot(
        jnp.concatenate([flat[2 * c, p] for c in range(2) for p in range(planes)], axis=1),
        gather_ref[...],
    ).astype(BF)

    y_up = pltpu.make_async_remote_copy(
        ysend_buf, ylo_buf, ys_sem.at[0], yr_sem.at[0],
        device_id=(me, lax.rem(mw + 1, wall_count)), device_id_type=MESH,
    )
    y_down = pltpu.make_async_remote_copy(
        ysend_buf, yhi_buf, ys_sem.at[1], yr_sem.at[1],
        device_id=(me, lax.rem(mw + wall_count - 1, wall_count)), device_id_type=MESH,
    )

    @pl.when(mw < wall_count - 1)
    def _():
        y_up.start()

    @pl.when(mw > 0)
    def _():
        y_down.start()

    @pl.when(mw == 0)
    def _():
        ylo_buf[...] = jnp.zeros_like(ylo_buf)

    @pl.when(mw == wall_count - 1)
    def _():
        yhi_buf[...] = jnp.zeros_like(yhi_buf)

    def along_x(k, carry):
        at = pl.ds(k * 4, 4)
        out = pl.ds(pl.multiple_of(k * 4 * cells, 4 * cells), 4 * cells)
        for c, buf in enumerate((v_buf, w_buf)):
            f = [buf[at, q].astype(F32) for q in range(6 + planes)]
            for p in range(planes):
                d = (
                    45.0 * (f[p + 4] - f[p + 2]) - 9.0 * (f[p + 5] - f[p + 1])
                    + (f[p + 6] - f[p])
                ).reshape(4 * cells, lanes)
                if c == 0:
                    acc[2, p, out] = d
                else:
                    acc[1, p, out] = -d
        return carry

    lax.fori_loop(0, snaps // 4, along_x, 0)

    if phases > 0:
        hear(0)
    if phases > 1:
        tell(1)

    @pl.when(mw > 0)
    def _():
        y_up.wait_recv()

    @pl.when(mw < wall_count - 1)
    def _():
        y_down.wait_recv()

    sides = jnp.concatenate([ylo_buf[...], yhi_buf[...]], axis=1)
    metric = metric_ref[...]
    for c in range(2):
        for p in range(planes):
            for k in range(2):
                g = (c * planes + p) * 2 + k
                at = slice(k * rows, (k + 1) * rows)
                f = flat[2 * c, p, :, k * lanes : (k + 1) * lanes]
                d = dot(f, wall_ref[...])
                d = d + dot(sides, scatter_ref[:, g * lanes : (g + 1) * lanes])
                d = d * metric
                if c == 0:
                    acc[2, p, at] = acc[2, p, at] - d
                else:
                    acc[0, p, at] = d

    def finish(comp, p, k, value):
        slab = comp * planes + p
        at = slice(k * rows, (k + 1) * rows)
        v = (value * (1.0 / 60.0)).astype(BF)
        vort[at, slab * lanes : (slab + 1) * lanes] = v
        vz[slab % 2, at] = v.astype(F32)

    def gram_of(slab):
        a = jnp.concatenate(
            [vz[slab % 2, pl.ds(z, snaps, stride=cells), :].astype(BF) for z in range(cells)],
            axis=1,
        )
        return lax.dot_general(
            a, jnp.concatenate([a, a], axis=0), (((1,), (1,)), ((), ())),
            preferred_element_type=F32,
        )

    for p in range(planes):
        for c in range(2):
            d = dot(inside_ref[...], flat[c, p])
            for k in range(2):
                at = slice(k * rows, (k + 1) * rows)
                part = d[:, k * lanes : (k + 1) * lanes]
                if c == 0:
                    acc[1, p, at] = acc[1, p, at] + part
                else:
                    acc[0, p, at] = acc[0, p, at] - part
    g = None
    for p in range(planes):
        for k in range(2):
            finish(2, p, k, acc[2, p, k * rows : (k + 1) * rows])
        part = gram_of(2 * planes + p)
        g = part if g is None else g + part
    if phases > 1:
        hear(1)
    for phase in range(2, phases):
        tell(phase)
        if phase < phases - 1:
            hear(phase)

    for c in range(2):
        for p in range(planes):
            for copy in halo[c * planes + p]:
                copy.wait_recv()
            d = dot(outside_ref[...], halo_buf[c, p])
            for k in range(2):
                at = slice(k * rows, (k + 1) * rows)
                part = d[:, k * lanes : (k + 1) * lanes]
                if c == 0:
                    finish(1, p, k, acc[1, p, at] + part)
                else:
                    finish(0, p, k, acc[0, p, at] - part)
            g = g + gram_of((1 - c) * planes + p)
    if phases > 2:
        hear(phases - 1)

    lane = lax.broadcasted_iota(jnp.int32, (half, 2 * snaps), 1)
    packed = jnp.where(lane < snaps, g[:half], g[half:])
    each = half // wall_count
    copies = []

    def remote(src, dst, send, recv, device):
        copy = pltpu.make_async_remote_copy(
            src, dst, send, recv, device_id=device, device_id_type=MESH
        )
        copy.start()
        return copy

    for w in range(wall_count):
        stage[w] = packed[w * each : (w + 1) * each]
    piece_buf[mw] = stage[mw]
    started = []
    for d in range(1, wall_count):
        w = lax.rem(mw + d, wall_count)
        started.append(
            remote(stage.at[w], piece_buf.at[mw], ps_sem.at[d], pr_sem.at[d], (me, w))
        )
    for copy in started:
        copy.wait_recv()
    copies += started
    total = piece_buf[0]
    for w in range(1, wall_count):
        total = total + piece_buf[w]
    sum_buf[me] = total
    started = []
    for d in range(1, span_count):
        started.append(
            remote(sum_buf.at[me], sum_buf.at[me], ss_sem.at[d], sr_sem.at[d], (ring(d), mw))
        )
    for copy in started:
        copy.wait_recv()
    copies += started
    total = sum_buf[0]
    for i in range(1, span_count):
        total = total + sum_buf[i]
    full_buf[mw] = total / total_rows
    started = []
    for d in range(1, wall_count):
        w = lax.rem(mw + d, wall_count)
        started.append(
            remote(full_buf.at[mw], full_buf.at[mw], fs_sem.at[d], fr_sem.at[d], (me, w))
        )
    for copy in started:
        copy.wait_recv()
    copies += started
    for w in range(wall_count):
        gram_ref[w * each : (w + 1) * each] = full_buf[w]

    for copy in copies:
        copy.wait_send()
    for pair in halo:
        for copy in pair:
            copy.wait_send()

    @pl.when(mw < wall_count - 1)
    def _():
        y_up.wait_send()

    @pl.when(mw > 0)
    def _():
        y_down.wait_send()


def modes_kernel(vort, gram_ref, spread_ref, out_hbm, r_hbm, out, r_ref, sem):
    snaps, comps, planes, cells, lanes = out.shape
    half = snaps // 2
    gram = gram_ref[...]
    lane = lax.broadcasted_iota(jnp.int32, (half, 2 * snaps), 1)
    sub = lax.broadcasted_iota(jnp.int32, (half, 2 * snaps), 0)
    top = jnp.where(lane < snaps, gram, (lane - snaps == sub).astype(F32))
    bottom = jnp.where(
        lane < snaps, pltpu.roll(gram, snaps, 1), (lane - snaps - half == sub).astype(F32)
    )
    groups = [top[8 * i : 8 * i + 8] for i in range(half // 8)]
    groups += [bottom[8 * i : 8 * i + 8] for i in range(half // 8)]
    lane8 = lax.broadcasted_iota(jnp.int32, (8, 2 * snaps), 1)
    sub8 = lax.broadcasted_iota(jnp.int32, (8, 2 * snaps), 0)
    count = 2
    block = 8 * count
    wide = block * cells
    row_z = lax.rem(lax.broadcasted_iota(jnp.int32, (wide, snaps * cells), 0), cells)
    col_z = lax.rem(lax.broadcasted_iota(jnp.int32, (wide, snaps * cells), 1), cells)
    same = row_z == col_z
    scaled = []
    stores = []
    for b, (p, s) in enumerate(eliminate(groups)):
        q = [p[k] / jnp.sqrt(s[k]) for k in range(8)]
        row = q[0]
        for k in range(1, 8):
            row = jnp.where(sub8 == k, q[k], row)
        row = jnp.where(lane8 < sub8 + 8 * b, 0.0, row)
        r_ref[8 * b : 8 * b + 8] = row[:, :snaps]
        scaled += q
        if b % count == count - 1:
            x = jnp.concatenate(scaled, axis=0).astype(BF)
            scaled = []
            n = b // count
            depth = (n + 1) * wide
            w = dot(x, spread_ref[:, :depth])
            w = jnp.where(same[:, :depth], w, 0.0).astype(BF)
            m = dot(w, vort[:depth])
            at = pl.ds(n * block, block)
            for comp in range(comps):
                for p_ in range(planes):
                    slab = comp * planes + p_
                    out[n * block : (n + 1) * block, comp, p_] = (
                        m[:, slab * lanes : (slab + 1) * lanes]
                        .reshape(block, cells, lanes).astype(BF)
                    )
            store = pltpu.make_async_copy(out.at[at], out_hbm.at[at], sem.at[n])
            store.start()
            stores.append(store)
    store = pltpu.make_async_copy(r_ref, r_hbm, sem.at[4])
    store.start()
    stores.append(store)
    for store in stores:
        store.wait()


def per_device(velocity, wall_metric):
    snaps, comps, depth, cells, lanes = velocity.shape
    planes = depth - 6
    spans, walls = lax.axis_size("span"), lax.axis_size("wall")
    phases, reach = 0, 1
    while 2 * reach < spans:
        phases, reach = phases + 1, 2 * reach
    total_rows = 3 * planes * cells * spans * lanes * walls
    *consts, spread = constants(snaps, cells, lanes, planes)
    vmem = pl.BlockSpec(memory_space=pltpu.VMEM)
    hbm = pl.BlockSpec(memory_space=pl.ANY)
    dma = pltpu.SemaphoreType.DMA
    half = snaps // 2
    each = half // walls
    wide = snaps * cells
    rows = half * cells
    edge = half * 3
    slabs = comps * planes
    vorticity, gram = pl.pallas_call(
        functools.partial(kernel, spans, walls, total_rows),
        out_shape=(
            pltpu.VMEM((wide, slabs * lanes), BF),
            pltpu.VMEM((half, 2 * snaps), F32),
        ),
        in_specs=[hbm] * (2 + len(consts)),
        out_specs=(vmem, vmem),
        scratch_shapes=[
            pltpu.VMEM((1, lanes), F32),
            *[pltpu.VMEM(a.shape, a.dtype) for a in consts],
            pltpu.VMEM((snaps, planes, cells, lanes), BF),
            pltpu.VMEM((snaps, depth, cells, lanes), BF),
            pltpu.VMEM((snaps, depth, cells, lanes), BF),
            pltpu.VMEM((3, planes, rows, 2 * lanes), BF),
            pltpu.VMEM((2, planes, 2 * edge, 2 * lanes), BF),
            pltpu.VMEM((2, planes, 2 * edge, 2 * lanes), BF),
            pltpu.VMEM((rows, lanes), BF),
            pltpu.VMEM((rows, lanes), BF),
            pltpu.VMEM((rows, lanes), BF),
            pltpu.VMEM((3, planes, wide, lanes), F32),
            pltpu.VMEM((2, wide, lanes), F32),
            pltpu.VMEM((walls, each, 2 * snaps), F32),
            pltpu.VMEM((walls, each, 2 * snaps), F32),
            pltpu.VMEM((spans, each, 2 * snaps), F32),
            pltpu.VMEM((walls, each, 2 * snaps), F32),
            dma((12,)),
            dma((2, planes, 2)),
            dma((2, planes, 2)),
            dma((2,)),
            dma((2,)),
            dma((walls,)),
            dma((walls,)),
            dma((spans,)),
            dma((spans,)),
            dma((walls,)),
            dma((walls,)),
            pltpu.SemaphoreType.REGULAR((phases,)),
        ],
        compiler_params=pltpu.CompilerParams(
            collective_id=0, has_side_effects=True, vmem_limit_bytes=60 << 20
        ),
        name="pod",
    )(velocity, wall_metric.reshape(1, lanes), *consts)
    return pl.pallas_call(
        modes_kernel,
        out_shape=(
            jax.ShapeDtypeStruct((snaps, comps, planes, cells, lanes), BF),
            jax.ShapeDtypeStruct((snaps, snaps), F32),
        ),
        in_specs=[vmem, vmem, vmem],
        out_specs=(hbm, hbm),
        scratch_shapes=[
            pltpu.VMEM((snaps, comps, planes, cells, lanes), BF),
            pltpu.VMEM((snaps, snaps), F32),
            dma((5,)),
        ],
        compiler_params=pltpu.CompilerParams(vmem_limit_bytes=32 << 20),
        name="modes",
    )(vorticity, gram, spread)


def solution(mesh):
    in_specs = (P(None, None, None, "span", "wall"), P("wall"))
    out_specs = (P(None, None, None, "span", "wall"), P())
    return jax.shard_map(
        per_device, mesh=mesh, in_specs=in_specs, out_specs=out_specs, check_vma=False
    )
```

```python
import functools

import jax
import jax.numpy as jnp
import ml_dtypes
import numpy as np
from jax import lax
from jax.experimental import pallas as pl
from jax.experimental.pallas import tpu as pltpu
from jax.sharding import PartitionSpec as P

MESH = pl.DeviceIdType.MESH
BF = jnp.bfloat16
F32 = jnp.float32


def coef(offset):
    table = {1: 45.0, 2: -9.0, 3: 1.0}
    size = np.abs(offset)
    out = np.zeros(offset.shape, np.float32)
    for step, value in table.items():
        out = np.where(size == step, value * np.sign(offset), out)
    return out


def constants(snaps, cells, lanes, planes):
    half = snaps // 2
    z = np.arange(cells)
    r = np.arange(3)
    eye = np.eye(half, dtype=np.float32)
    pick = np.concatenate(
        [
            np.kron(eye, (z[None, :] == r[:, None]).astype(np.float32)),
            np.kron(eye, (z[None, :] == cells - 3 + r[:, None]).astype(np.float32)),
        ],
        axis=0,
    )
    inside = np.kron(eye, coef(z[None, :] - z[:, None]))
    outside = np.concatenate(
        [
            np.kron(eye, coef(r[None, :] - 3 - z[:, None])),
            np.kron(eye, coef(cells + r[None, :] - z[:, None])),
        ],
        axis=1,
    )
    y = np.arange(lanes)
    wall = coef(y[:, None] - y[None, :])
    packs = 4 * planes
    step = lanes // packs
    gather = np.zeros((packs, lanes, lanes), np.float32)
    scatter = np.zeros((2, lanes, packs, lanes), np.float32)
    for g in range(packs):
        for t in range(3):
            gather[g, t, g * step + t] = 1.0
            gather[g, lanes - 3 + t, g * step + 3 + t] = 1.0
            scatter[0, g * step + 3 + t, g] = coef(t - 3 - y)
            scatter[1, g * step + t, g] = coef(lanes + t - y)
    gather = gather.reshape(packs * lanes, lanes)
    scatter = scatter.reshape(2 * lanes, packs * lanes)
    owner = np.arange(snaps * cells) // cells
    one = (owner[None, :] == np.arange(snaps)[:, None]).astype(np.float32)
    spread = np.concatenate([np.zeros_like(one), one], axis=0)
    tables = (pick, inside, outside, gather, wall, scatter, spread)
    return [jnp.asarray(a.astype(ml_dtypes.bfloat16)) for a in tables]


def dot(a, b):
    return jnp.dot(a, b, preferred_element_type=F32)


def eliminate(rows):
    groups = list(rows)
    count = len(groups)
    sub = lax.broadcasted_iota(jnp.int32, (8, 128), 0)

    def wide(value):
        return jnp.broadcast_to(value, (8, 128))

    for b in range(count):
        at = 8 * b
        p = [wide(groups[b][k : k + 1, :]) for k in range(8)]
        s = {(k, l): wide(p[k][:, at + l : at + l + 1]) for k in range(8) for l in range(k, 8)}
        inv, f = [], {}
        for k in range(8):
            inv.append(1.0 / s[k, k])
            for l in range(k + 1, 8):
                f[k, l] = s[k, l] * inv[k]
                for m in range(l, 8):
                    s[l, m] = s[l, m] - f[k, l] * s[k, m]
        for k in range(8):
            for l in range(k + 1, 8):
                p[l] = p[l] - f[k, l] * p[k]
        scaled = [p[k] * inv[k] for k in range(8)]
        for i in range(b + 1, count):
            c = [wide(groups[i][:, at + k : at + k + 1]) for k in range(8)]
            value = groups[i]
            for k in range(8):
                for l in range(k + 1, 8):
                    c[l] = c[l] - c[k] * f[k, l]
                value = value - c[k] * scaled[k]
            groups[i] = value
        yield p, [s[k, k] for k in range(8)]


def kernel(
    span_count, wall_count, total_rows,
    vel, metric_hbm, pick_hbm, inside_hbm, outside_hbm, gather_hbm, wall_hbm, scatter_hbm,
    vort, gram_ref,
    metric_ref, pick_ref, inside_ref, outside_ref, gather_ref, wall_ref, scatter_ref,
    u_buf, v_buf, w_buf, flat, send_buf, halo_buf, ysend_buf, ylo_buf, yhi_buf, acc, vz,
    stage, piece_buf, sum_buf, full_buf,
    local_sem, hs_sem, hr_sem, ys_sem, yr_sem, ps_sem, pr_sem, ss_sem, sr_sem, fs_sem, fr_sem, seen,
):
    snaps, planes = u_buf.shape[0], u_buf.shape[1]
    cells, lanes = vel.shape[3], vel.shape[4]
    half = snaps // 2
    rows = half * cells
    edge = half * 3
    me = lax.axis_index("span")
    mw = lax.axis_index("wall")

    def ring(d):
        return lax.rem(me + span_count + d, span_count)

    down, up = ring(-1), ring(1)

    def load(i, src, dst):
        copy = pltpu.make_async_copy(src, dst, local_sem.at[i])
        copy.start()
        return copy

    mid = pl.ds(3, planes)
    load_pick = load(0, pick_hbm, pick_ref)
    load_u = load(1, vel.at[:, 0, mid], u_buf)
    load_v = load(2, vel.at[:, 1, mid], v_buf.at[:, mid])
    load_rest = [
        load(3, gather_hbm, gather_ref),
        load(4, vel.at[:, 2], w_buf),
        load(5, vel.at[:, 1, pl.ds(0, 3)], v_buf.at[:, pl.ds(0, 3)]),
        load(6, vel.at[:, 1, pl.ds(3 + planes, 3)], v_buf.at[:, pl.ds(3 + planes, 3)]),
        load(7, wall_hbm, wall_ref),
        load(8, scatter_hbm, scatter_ref),
        load(9, metric_hbm, metric_ref),
        load(10, inside_hbm, inside_ref),
        load(11, outside_hbm, outside_ref),
    ]

    barrier = pltpu.get_barrier_semaphore()
    for peer in (down, up):
        pl.semaphore_signal(barrier, inc=1, device_id=(peer, mw), device_id_type=MESH)
    for d in range(1, wall_count):
        pl.semaphore_signal(
            barrier, inc=1, device_id=(me, lax.rem(mw + d, wall_count)), device_id_type=MESH
        )

    def tell(phase):
        for peer in (ring(-(1 << phase)), ring(1 << phase)):
            pl.semaphore_signal(seen.at[phase], inc=1, device_id=(peer, mw), device_id_type=MESH)

    def hear(phase):
        pl.semaphore_wait(seen.at[phase], 2)

    def rows_of(value):
        return value.astype(F32).reshape(rows, lanes).astype(BF)

    def wide(buf, p):
        return jnp.concatenate(
            [rows_of(buf[k * half : (k + 1) * half, p]) for k in range(2)], axis=1
        )

    odd = lax.rem(me, 2)

    def piece(c, p, turn):
        side = 1 - odd if turn == 0 else odd
        here = pl.multiple_of(side * edge, edge)
        there = pl.multiple_of((1 - side) * edge, edge)
        return pltpu.make_async_remote_copy(
            send_buf.at[c, p, pl.ds(here, edge)], halo_buf.at[c, p, pl.ds(there, edge)],
            hs_sem.at[c, p, side], hr_sem.at[c, p, side],
            device_id=(ring(2 * side - 1), mw), device_id_type=MESH,
        )

    halo = []
    for c in range(2):
        if c == 0:
            load_pick.wait()
            load_u.wait()
        else:
            load_v.wait()
        for p in range(planes):
            f = wide(u_buf, p) if c == 0 else wide(v_buf, 3 + p)
            flat[c, p] = f
            send_buf[c, p] = dot(pick_ref[...], f).astype(BF)
            if c == 0 and p == 0:
                pl.semaphore_wait(barrier, 2 + wall_count - 1)
            halo.append([piece(c, p, turn) for turn in range(2)])
            halo[-1][0].start()
    for pair in halo:
        pair[1].start()

    phases = seen.shape[0]
    tell(0)
    for copy in load_rest:
        copy.wait()
    for p in range(planes):
        flat[2, p] = wide(w_buf, 3 + p)
    ysend_buf[...] = dot(
        jnp.concatenate([flat[2 * c, p] for c in range(2) for p in range(planes)], axis=1),
        gather_ref[...],
    ).astype(BF)

    y_up = pltpu.make_async_remote_copy(
        ysend_buf, ylo_buf, ys_sem.at[0], yr_sem.at[0],
        device_id=(me, lax.rem(mw + 1, wall_count)), device_id_type=MESH,
    )
    y_down = pltpu.make_async_remote_copy(
        ysend_buf, yhi_buf, ys_sem.at[1], yr_sem.at[1],
        device_id=(me, lax.rem(mw + wall_count - 1, wall_count)), device_id_type=MESH,
    )

    @pl.when(mw < wall_count - 1)
    def _():
        y_up.start()

    @pl.when(mw > 0)
    def _():
        y_down.start()

    @pl.when(mw == 0)
    def _():
        ylo_buf[...] = jnp.zeros_like(ylo_buf)

    @pl.when(mw == wall_count - 1)
    def _():
        yhi_buf[...] = jnp.zeros_like(yhi_buf)

    def along_x(k, carry):
        at = pl.ds(k * 4, 4)
        out = pl.ds(pl.multiple_of(k * 4 * cells, 4 * cells), 4 * cells)
        for c, buf in enumerate((v_buf, w_buf)):
            f = [buf[at, q].astype(F32) for q in range(6 + planes)]
            for p in range(planes):
                d = (
                    45.0 * (f[p + 4] - f[p + 2]) - 9.0 * (f[p + 5] - f[p + 1])
                    + (f[p + 6] - f[p])
                ).reshape(4 * cells, lanes)
                if c == 0:
                    acc[2, p, out] = d
                else:
                    acc[1, p, out] = -d
        return carry

    lax.fori_loop(0, snaps // 4, along_x, 0)

    if phases > 0:
        hear(0)
    if phases > 1:
        tell(1)

    @pl.when(mw > 0)
    def _():
        y_up.wait_recv()

    @pl.when(mw < wall_count - 1)
    def _():
        y_down.wait_recv()

    sides = jnp.concatenate([ylo_buf[...], yhi_buf[...]], axis=1)
    metric = metric_ref[...]
    for c in range(2):
        for p in range(planes):
            for k in range(2):
                g = (c * planes + p) * 2 + k
                at = slice(k * rows, (k + 1) * rows)
                f = flat[2 * c, p, :, k * lanes : (k + 1) * lanes]
                d = dot(f, wall_ref[...])
                d = d + dot(sides, scatter_ref[:, g * lanes : (g + 1) * lanes])
                d = d * metric
                if c == 0:
                    acc[2, p, at] = acc[2, p, at] - d
                else:
                    acc[0, p, at] = d

    def finish(comp, p, k, value):
        slab = comp * planes + p
        at = slice(k * rows, (k + 1) * rows)
        v = (value * (1.0 / 60.0)).astype(BF)
        vort[at, slab * lanes : (slab + 1) * lanes] = v
        vz[slab % 2, at] = v.astype(F32)

    def gram_of(slab):
        a = jnp.concatenate(
            [vz[slab % 2, pl.ds(z, snaps, stride=cells), :].astype(BF) for z in range(cells)],
            axis=1,
        )
        return lax.dot_general(
            a, jnp.concatenate([a, a], axis=0), (((1,), (1,)), ((), ())),
            preferred_element_type=F32,
        )

    for p in range(planes):
        for c in range(2):
            d = dot(inside_ref[...], flat[c, p])
            for k in range(2):
                at = slice(k * rows, (k + 1) * rows)
                part = d[:, k * lanes : (k + 1) * lanes]
                if c == 0:
                    acc[1, p, at] = acc[1, p, at] + part
                else:
                    acc[0, p, at] = acc[0, p, at] - part
    g = None
    for p in range(planes):
        for k in range(2):
            finish(2, p, k, acc[2, p, k * rows : (k + 1) * rows])
        part = gram_of(2 * planes + p)
        g = part if g is None else g + part
    if phases > 1:
        hear(1)
    for phase in range(2, phases):
        tell(phase)
        if phase < phases - 1:
            hear(phase)

    for c in range(2):
        for p in range(planes):
            for copy in halo[c * planes + p]:
                copy.wait_recv()
            d = dot(outside_ref[...], halo_buf[c, p])
            for k in range(2):
                at = slice(k * rows, (k + 1) * rows)
                part = d[:, k * lanes : (k + 1) * lanes]
                if c == 0:
                    finish(1, p, k, acc[1, p, at] + part)
                else:
                    finish(0, p, k, acc[0, p, at] - part)
            g = g + gram_of((1 - c) * planes + p)
    if phases > 2:
        hear(phases - 1)

    lane = lax.broadcasted_iota(jnp.int32, (half, 2 * snaps), 1)
    packed = jnp.where(lane < snaps, g[:half], g[half:])
    each = half // wall_count
    copies = []

    def remote(src, dst, send, recv, device):
        copy = pltpu.make_async_remote_copy(
            src, dst, send, recv, device_id=device, device_id_type=MESH
        )
        copy.start()
        return copy

    for w in range(wall_count):
        stage[w] = packed[w * each : (w + 1) * each]
    piece_buf[mw] = stage[mw]
    started = []
    for d in range(1, wall_count):
        w = lax.rem(mw + d, wall_count)
        started.append(
            remote(stage.at[w], piece_buf.at[mw], ps_sem.at[d], pr_sem.at[d], (me, w))
        )
    for copy in started:
        copy.wait_recv()
    copies += started
    total = piece_buf[0]
    for w in range(1, wall_count):
        total = total + piece_buf[w]
    sum_buf[me] = total
    started = []
    for d in range(1, span_count):
        started.append(
            remote(sum_buf.at[me], sum_buf.at[me], ss_sem.at[d], sr_sem.at[d], (ring(d), mw))
        )
    for copy in started:
        copy.wait_recv()
    copies += started
    total = sum_buf[0]
    for i in range(1, span_count):
        total = total + sum_buf[i]
    full_buf[mw] = total / total_rows
    started = []
    for d in range(1, wall_count):
        w = lax.rem(mw + d, wall_count)
        started.append(
            remote(full_buf.at[mw], full_buf.at[mw], fs_sem.at[d], fr_sem.at[d], (me, w))
        )
    for copy in started:
        copy.wait_recv()
    copies += started
    for w in range(wall_count):
        gram_ref[w * each : (w + 1) * each] = full_buf[w]

    for copy in copies:
        copy.wait_send()
    for pair in halo:
        for copy in pair:
            copy.wait_send()

    @pl.when(mw < wall_count - 1)
    def _():
        y_up.wait_send()

    @pl.when(mw > 0)
    def _():
        y_down.wait_send()


def modes_kernel(vort, gram_ref, spread_ref, out_hbm, r_hbm, out, r_ref, sem):
    snaps, comps, planes, cells, lanes = out.shape
    half = snaps // 2
    gram = gram_ref[...]
    lane = lax.broadcasted_iota(jnp.int32, (half, 2 * snaps), 1)
    sub = lax.broadcasted_iota(jnp.int32, (half, 2 * snaps), 0)
    top = jnp.where(lane < snaps, gram, (lane - snaps == sub).astype(F32))
    bottom = jnp.where(
        lane < snaps, pltpu.roll(gram, snaps, 1), (lane - snaps - half == sub).astype(F32)
    )
    groups = [top[8 * i : 8 * i + 8] for i in range(half // 8)]
    groups += [bottom[8 * i : 8 * i + 8] for i in range(half // 8)]
    lane8 = lax.broadcasted_iota(jnp.int32, (8, 2 * snaps), 1)
    sub8 = lax.broadcasted_iota(jnp.int32, (8, 2 * snaps), 0)
    count = 2
    block = 8 * count
    wide = block * cells
    row_z = lax.rem(lax.broadcasted_iota(jnp.int32, (wide, snaps * cells), 0), cells)
    col_z = lax.rem(lax.broadcasted_iota(jnp.int32, (wide, snaps * cells), 1), cells)
    same = row_z == col_z
    scaled = []
    stores = []
    for b, (p, s) in enumerate(eliminate(groups)):
        q = [p[k] / jnp.sqrt(s[k]) for k in range(8)]
        row = q[0]
        for k in range(1, 8):
            row = jnp.where(sub8 == k, q[k], row)
        row = jnp.where(lane8 < sub8 + 8 * b, 0.0, row)
        r_ref[8 * b : 8 * b + 8] = row[:, :snaps]
        scaled += q
        if b % count == count - 1:
            x = jnp.concatenate(scaled, axis=0).astype(BF)
            scaled = []
            n = b // count
            depth = (n + 1) * wide
            w = dot(x, spread_ref[:, :depth])
            w = jnp.where(same[:, :depth], w, 0.0).astype(BF)
            m = dot(w, vort[:depth])
            at = pl.ds(n * block, block)
            for comp in range(comps):
                for p_ in range(planes):
                    slab = comp * planes + p_
                    out[n * block : (n + 1) * block, comp, p_] = (
                        m[:, slab * lanes : (slab + 1) * lanes]
                        .reshape(block, cells, lanes).astype(BF)
                    )
            store = pltpu.make_async_copy(out.at[at], out_hbm.at[at], sem.at[n])
            store.start()
            stores.append(store)
    store = pltpu.make_async_copy(r_ref, r_hbm, sem.at[4])
    store.start()
    stores.append(store)
    for store in stores:
        store.wait()


def per_device(velocity, wall_metric):
    snaps, comps, depth, cells, lanes = velocity.shape
    planes = depth - 6
    spans, walls = lax.axis_size("span"), lax.axis_size("wall")
    phases, reach = 0, 1
    while 2 * reach < spans:
        phases, reach = phases + 1, 2 * reach
    total_rows = 3 * planes * cells * spans * lanes * walls
    *consts, spread = constants(snaps, cells, lanes, planes)
    vmem = pl.BlockSpec(memory_space=pltpu.VMEM)
    hbm = pl.BlockSpec(memory_space=pl.ANY)
    dma = pltpu.SemaphoreType.DMA
    half = snaps // 2
    each = half // walls
    wide = snaps * cells
    rows = half * cells
    edge = half * 3
    slabs = comps * planes
    vorticity, gram = pl.pallas_call(
        functools.partial(kernel, spans, walls, total_rows),
        out_shape=(
            pltpu.VMEM((wide, slabs * lanes), BF),
            pltpu.VMEM((half, 2 * snaps), F32),
        ),
        in_specs=[hbm] * (2 + len(consts)),
        out_specs=(vmem, vmem),
        scratch_shapes=[
            pltpu.VMEM((1, lanes), F32),
            *[pltpu.VMEM(a.shape, a.dtype) for a in consts],
            pltpu.VMEM((snaps, planes, cells, lanes), BF),
            pltpu.VMEM((snaps, depth, cells, lanes), BF),
            pltpu.VMEM((snaps, depth, cells, lanes), BF),
            pltpu.VMEM((3, planes, rows, 2 * lanes), BF),
            pltpu.VMEM((2, planes, 2 * edge, 2 * lanes), BF),
            pltpu.VMEM((2, planes, 2 * edge, 2 * lanes), BF),
            pltpu.VMEM((rows, lanes), BF),
            pltpu.VMEM((rows, lanes), BF),
            pltpu.VMEM((rows, lanes), BF),
            pltpu.VMEM((3, planes, wide, lanes), F32),
            pltpu.VMEM((2, wide, lanes), F32),
            pltpu.VMEM((walls, each, 2 * snaps), F32),
            pltpu.VMEM((walls, each, 2 * snaps), F32),
            pltpu.VMEM((spans, each, 2 * snaps), F32),
            pltpu.VMEM((walls, each, 2 * snaps), F32),
            dma((12,)),
            dma((2, planes, 2)),
            dma((2, planes, 2)),
            dma((2,)),
            dma((2,)),
            dma((walls,)),
            dma((walls,)),
            dma((spans,)),
            dma((spans,)),
            dma((walls,)),
            dma((walls,)),
            pltpu.SemaphoreType.REGULAR((phases,)),
        ],
        compiler_params=pltpu.CompilerParams(
            collective_id=0, has_side_effects=True, vmem_limit_bytes=60 << 20
        ),
        name="pod",
    )(velocity, wall_metric.reshape(1, lanes), *consts)
    return pl.pallas_call(
        modes_kernel,
        out_shape=(
            jax.ShapeDtypeStruct((snaps, comps, planes, cells, lanes), BF),
            jax.ShapeDtypeStruct((snaps, snaps), F32),
        ),
        in_specs=[vmem, vmem, vmem],
        out_specs=(hbm, hbm),
        scratch_shapes=[
            pltpu.VMEM((snaps, comps, planes, cells, lanes), BF),
            pltpu.VMEM((snaps, snaps), F32),
            dma((5,)),
        ],
        compiler_params=pltpu.CompilerParams(vmem_limit_bytes=32 << 20),
        name="modes",
    )(vorticity, gram, spread)


def solution(mesh):
    in_specs = (P(None, None, None, "span", "wall"), P("wall"))
    out_specs = (P(None, None, None, "span", "wall"), P())
    return jax.shard_map(
        per_device, mesh=mesh, in_specs=in_specs, out_specs=out_specs, check_vma=False
    )
```

```python
import functools

import jax
import jax.numpy as jnp
import ml_dtypes
import numpy as np
from jax import lax
from jax.experimental import pallas as pl
from jax.experimental.pallas import tpu as pltpu
from jax.sharding import PartitionSpec as P

MESH = pl.DeviceIdType.MESH
BF = jnp.bfloat16
F32 = jnp.float32


def coef(offset):
    table = {1: 45.0, 2: -9.0, 3: 1.0}
    size = np.abs(offset)
    out = np.zeros(offset.shape, np.float32)
    for step, value in table.items():
        out = np.where(size == step, value * np.sign(offset), out)
    return out


def constants(snaps, cells, lanes, planes):
    half = snaps // 2
    z = np.arange(cells)
    r = np.arange(3)
    eye = np.eye(half, dtype=np.float32)
    pick = np.concatenate(
        [
            np.kron(eye, (z[None, :] == r[:, None]).astype(np.float32)),
            np.kron(eye, (z[None, :] == cells - 3 + r[:, None]).astype(np.float32)),
        ],
        axis=0,
    )
    inside = np.kron(eye, coef(z[None, :] - z[:, None]))
    outside = np.concatenate(
        [
            np.kron(eye, coef(r[None, :] - 3 - z[:, None])),
            np.kron(eye, coef(cells + r[None, :] - z[:, None])),
        ],
        axis=1,
    )
    y = np.arange(lanes)
    wall = coef(y[:, None] - y[None, :])
    packs = 4 * planes
    step = lanes // packs
    gather = np.zeros((packs, lanes, lanes), np.float32)
    scatter = np.zeros((2, lanes, packs, lanes), np.float32)
    for g in range(packs):
        for t in range(3):
            gather[g, t, g * step + t] = 1.0
            gather[g, lanes - 3 + t, g * step + 3 + t] = 1.0
            scatter[0, g * step + 3 + t, g] = coef(t - 3 - y)
            scatter[1, g * step + t, g] = coef(lanes + t - y)
    gather = gather.reshape(packs * lanes, lanes)
    scatter = scatter.reshape(2 * lanes, packs * lanes)
    owner = np.arange(snaps * cells) // cells
    one = (owner[None, :] == np.arange(snaps)[:, None]).astype(np.float32)
    spread = np.concatenate([np.zeros_like(one), one], axis=0)
    tables = (pick, inside, outside, gather, wall, scatter, spread)
    return [jnp.asarray(a.astype(ml_dtypes.bfloat16)) for a in tables]


def dot(a, b):
    return jnp.dot(a, b, preferred_element_type=F32)


def eliminate(groups, start, stop):
    count = len(groups)
    sub = lax.broadcasted_iota(jnp.int32, (8, 128), 0)

    def wide(value):
        return jnp.broadcast_to(value, (8, 128))

    for b in range(start, stop):
        at = 8 * b
        p = [wide(groups[b][k : k + 1, :]) for k in range(8)]
        s = {(k, l): wide(p[k][:, at + l : at + l + 1]) for k in range(8) for l in range(k, 8)}
        inv, f = [], {}
        for k in range(8):
            inv.append(1.0 / s[k, k])
            for l in range(k + 1, 8):
                f[k, l] = s[k, l] * inv[k]
                for m in range(l, 8):
                    s[l, m] = s[l, m] - f[k, l] * s[k, m]
        for k in range(8):
            for l in range(k + 1, 8):
                p[l] = p[l] - f[k, l] * p[k]
        scaled = [p[k] * inv[k] for k in range(8)]
        for i in range(b + 1, count):
            c = [wide(groups[i][:, at + k : at + k + 1]) for k in range(8)]
            value = groups[i]
            for k in range(8):
                for l in range(k + 1, 8):
                    c[l] = c[l] - c[k] * f[k, l]
                value = value - c[k] * scaled[k]
            groups[i] = value
        yield p, [s[k, k] for k in range(8)]


def scaled_rows(p, s):
    sub = lax.broadcasted_iota(jnp.int32, (8, 128), 0)
    row = p[0] / jnp.sqrt(s[0])
    for k in range(1, 8):
        row = jnp.where(sub == k, p[k] / jnp.sqrt(s[k]), row)
    return row


def kernel(
    span_count, wall_count, total_rows,
    vel, metric_hbm, pick_hbm, inside_hbm, outside_hbm, gather_hbm, wall_hbm, scatter_hbm,
    vort, state_ref,
    metric_ref, pick_ref, inside_ref, outside_ref, gather_ref, wall_ref, scatter_ref,
    u_buf, v_buf, w_buf, flat, send_buf, halo_buf, ysend_buf, ylo_buf, yhi_buf, acc, vz,
    piece_buf, sum_buf,
    local_sem, hs_sem, hr_sem, ys_sem, yr_sem, ps_sem, pr_sem, ss_sem, sr_sem, seen,
):
    snaps, planes = u_buf.shape[0], u_buf.shape[1]
    cells, lanes = vel.shape[3], vel.shape[4]
    half = snaps // 2
    rows = half * cells
    edge = half * 3
    me = lax.axis_index("span")
    mw = lax.axis_index("wall")

    def ring(d):
        return lax.rem(me + span_count + d, span_count)

    down, up = ring(-1), ring(1)

    def load(i, src, dst):
        copy = pltpu.make_async_copy(src, dst, local_sem.at[i])
        copy.start()
        return copy

    mid = pl.ds(3, planes)
    load_pick = load(0, pick_hbm, pick_ref)
    load_u = load(1, vel.at[:, 0, mid], u_buf)
    load_v = load(2, vel.at[:, 1, mid], v_buf.at[:, mid])
    load_rest = [
        load(3, gather_hbm, gather_ref),
        load(4, vel.at[:, 2], w_buf),
        load(5, vel.at[:, 1, pl.ds(0, 3)], v_buf.at[:, pl.ds(0, 3)]),
        load(6, vel.at[:, 1, pl.ds(3 + planes, 3)], v_buf.at[:, pl.ds(3 + planes, 3)]),
        load(7, wall_hbm, wall_ref),
        load(8, scatter_hbm, scatter_ref),
        load(9, metric_hbm, metric_ref),
        load(10, inside_hbm, inside_ref),
        load(11, outside_hbm, outside_ref),
    ]

    barrier = pltpu.get_barrier_semaphore()
    for peer in (down, up):
        pl.semaphore_signal(barrier, inc=1, device_id=(peer, mw), device_id_type=MESH)
    for d in range(1, wall_count):
        pl.semaphore_signal(
            barrier, inc=1, device_id=(me, lax.rem(mw + d, wall_count)), device_id_type=MESH
        )

    def tell(phase):
        for peer in (ring(-(1 << phase)), ring(1 << phase)):
            pl.semaphore_signal(seen.at[phase], inc=1, device_id=(peer, mw), device_id_type=MESH)

    def hear(phase):
        pl.semaphore_wait(seen.at[phase], 2)

    def rows_of(value):
        return value.astype(F32).reshape(rows, lanes).astype(BF)

    def wide(buf, p):
        return jnp.concatenate(
            [rows_of(buf[k * half : (k + 1) * half, p]) for k in range(2)], axis=1
        )

    odd = lax.rem(me, 2)

    def piece(c, p, turn):
        side = 1 - odd if turn == 0 else odd
        here = pl.multiple_of(side * edge, edge)
        there = pl.multiple_of((1 - side) * edge, edge)
        return pltpu.make_async_remote_copy(
            send_buf.at[c, p, pl.ds(here, edge)], halo_buf.at[c, p, pl.ds(there, edge)],
            hs_sem.at[c, p, side], hr_sem.at[c, p, side],
            device_id=(ring(2 * side - 1), mw), device_id_type=MESH,
        )

    halo = []
    for c in range(2):
        if c == 0:
            load_pick.wait()
            load_u.wait()
        else:
            load_v.wait()
        for p in range(planes):
            f = wide(u_buf, p) if c == 0 else wide(v_buf, 3 + p)
            flat[c, p] = f
            send_buf[c, p] = dot(pick_ref[...], f).astype(BF)
            if c == 0 and p == 0:
                pl.semaphore_wait(barrier, 2 + wall_count - 1)
            halo.append([piece(c, p, turn) for turn in range(2)])
            halo[-1][0].start()
    for pair in halo:
        pair[1].start()

    phases = seen.shape[0]
    tell(0)
    for copy in load_rest:
        copy.wait()
    for p in range(planes):
        flat[2, p] = wide(w_buf, 3 + p)
    ysend_buf[...] = dot(
        jnp.concatenate([flat[2 * c, p] for c in range(2) for p in range(planes)], axis=1),
        gather_ref[...],
    ).astype(BF)

    y_up = pltpu.make_async_remote_copy(
        ysend_buf, ylo_buf, ys_sem.at[0], yr_sem.at[0],
        device_id=(me, lax.rem(mw + 1, wall_count)), device_id_type=MESH,
    )
    y_down = pltpu.make_async_remote_copy(
        ysend_buf, yhi_buf, ys_sem.at[1], yr_sem.at[1],
        device_id=(me, lax.rem(mw + wall_count - 1, wall_count)), device_id_type=MESH,
    )

    @pl.when(mw < wall_count - 1)
    def _():
        y_up.start()

    @pl.when(mw > 0)
    def _():
        y_down.start()

    @pl.when(mw == 0)
    def _():
        ylo_buf[...] = jnp.zeros_like(ylo_buf)

    @pl.when(mw == wall_count - 1)
    def _():
        yhi_buf[...] = jnp.zeros_like(yhi_buf)

    def along_x(k, carry):
        at = pl.ds(k * 4, 4)
        out = pl.ds(pl.multiple_of(k * 4 * cells, 4 * cells), 4 * cells)
        for c, buf in enumerate((v_buf, w_buf)):
            f = [buf[at, q].astype(F32) for q in range(6 + planes)]
            for p in range(planes):
                d = (
                    45.0 * (f[p + 4] - f[p + 2]) - 9.0 * (f[p + 5] - f[p + 1])
                    + (f[p + 6] - f[p])
                ).reshape(4 * cells, lanes)
                if c == 0:
                    acc[2, p, out] = d
                else:
                    acc[1, p, out] = -d
        return carry

    lax.fori_loop(0, snaps // 4, along_x, 0)

    if phases > 0:
        hear(0)
    if phases > 1:
        tell(1)

    @pl.when(mw > 0)
    def _():
        y_up.wait_recv()

    @pl.when(mw < wall_count - 1)
    def _():
        y_down.wait_recv()

    sides = jnp.concatenate([ylo_buf[...], yhi_buf[...]], axis=1)
    metric = metric_ref[...]
    for c in range(2):
        for p in range(planes):
            for k in range(2):
                g = (c * planes + p) * 2 + k
                at = slice(k * rows, (k + 1) * rows)
                f = flat[2 * c, p, :, k * lanes : (k + 1) * lanes]
                d = dot(f, wall_ref[...])
                d = d + dot(sides, scatter_ref[:, g * lanes : (g + 1) * lanes])
                d = d * metric
                if c == 0:
                    acc[2, p, at] = acc[2, p, at] - d
                else:
                    acc[0, p, at] = d

    def finish(comp, p, k, value):
        slab = comp * planes + p
        at = slice(k * rows, (k + 1) * rows)
        v = (value * (1.0 / 60.0)).astype(BF)
        vort[at, slab * lanes : (slab + 1) * lanes] = v
        vz[slab % 2, at] = v.astype(F32)

    def gram_of(slab):
        a = jnp.concatenate(
            [vz[slab % 2, pl.ds(z, snaps, stride=cells), :].astype(BF) for z in range(cells)],
            axis=1,
        )
        return lax.dot_general(
            a, jnp.concatenate([a, a], axis=0), (((1,), (1,)), ((), ())),
            preferred_element_type=F32,
        )

    for p in range(planes):
        for c in range(2):
            d = dot(inside_ref[...], flat[c, p])
            for k in range(2):
                at = slice(k * rows, (k + 1) * rows)
                part = d[:, k * lanes : (k + 1) * lanes]
                if c == 0:
                    acc[1, p, at] = acc[1, p, at] + part
                else:
                    acc[0, p, at] = acc[0, p, at] - part
    g = None
    for p in range(planes):
        for k in range(2):
            finish(2, p, k, acc[2, p, k * rows : (k + 1) * rows])
        part = gram_of(2 * planes + p)
        g = part if g is None else g + part
    if phases > 1:
        hear(1)
    for phase in range(2, phases):
        tell(phase)
        if phase < phases - 1:
            hear(phase)

    for c in range(2):
        for p in range(planes):
            for copy in halo[c * planes + p]:
                copy.wait_recv()
            d = dot(outside_ref[...], halo_buf[c, p])
            for k in range(2):
                at = slice(k * rows, (k + 1) * rows)
                part = d[:, k * lanes : (k + 1) * lanes]
                if c == 0:
                    finish(1, p, k, acc[1, p, at] + part)
                else:
                    finish(0, p, k, acc[0, p, at] - part)
            g = g + gram_of((1 - c) * planes + p)
    if phases > 2:
        hear(phases - 1)

    quarter = half // 2
    lane = lax.broadcasted_iota(jnp.int32, (8, 2 * snaps), 1)
    sub = lax.broadcasted_iota(jnp.int32, (8, 2 * snaps), 0)
    left = lane < snaps
    for i in range(quarter // 8):
        at = slice(8 * i, 8 * i + 8)
        piece_buf[mw, at] = jnp.where(left, g[at], g[quarter + 8 * i : quarter + 8 * i + 8])
    corner = None
    for i in range(4):
        part = g[half + 8 * i : half + 8 * i + 8]
        if i % 2 == 0:
            part = pltpu.roll(part, half, 1)
        corner = part if corner is None else jnp.where(lane < half * i, corner, part)
    piece_buf[mw, quarter : quarter + 8] = corner
    copies = []

    def remote(src, dst, send, recv, device):
        copy = pltpu.make_async_remote_copy(
            src, dst, send, recv, device_id=device, device_id_type=MESH
        )
        copy.start()
        return copy

    started = []
    for d in range(1, wall_count):
        w = lax.rem(mw + d, wall_count)
        started.append(
            remote(piece_buf.at[mw], piece_buf.at[mw], ps_sem.at[d], pr_sem.at[d], (me, w))
        )
    for copy in started:
        copy.wait_recv()
    copies += started
    total = piece_buf[0]
    for w in range(1, wall_count):
        total = total + piece_buf[w]
    sum_buf[me] = total
    others = [i + (me <= i).astype(jnp.int32) for i in range(span_count - 1)]
    parts = (pl.ds(0, quarter), pl.ds(quarter, 8))

    def to(turn, peer):
        mine = sum_buf.at[me, parts[turn]]
        copies.append(
            remote(mine, mine, ss_sem.at[turn, peer], sr_sem.at[turn, me], (peer, mw))
        )

    def arrived(turn):
        for peer in others:
            theirs = sum_buf.at[peer, parts[turn]]
            pltpu.make_async_remote_copy(
                theirs, theirs, ss_sem.at[turn, peer], sr_sem.at[turn, peer],
                device_id=(peer, mw), device_id_type=MESH,
            ).wait_recv()

    for peer in others:
        for turn in range(2):
            to(turn, peer)
    arrived(0)
    total = sum_buf[0, 0:quarter]
    for i in range(1, span_count):
        total = total + sum_buf[i, 0:quarter]
    total = total / total_rows
    top = jnp.concatenate([total, pltpu.roll(total, snaps, 1)], axis=0)
    turned = jnp.concatenate([top] * 4, axis=0).T
    groups = []
    for i in range(snaps // 8):
        if 8 * i < half:
            value = top[8 * i : 8 * i + 8]
        else:
            value = jnp.where(lane < half, turned[8 * i : 8 * i + 8], 0.0)
        groups.append(jnp.where(left, value, (lane - snaps - 8 * i == sub).astype(F32)))
    first = half // 8
    for b, (p, s) in enumerate(eliminate(groups, 0, first)):
        state_ref[8 * b : 8 * b + 8] = scaled_rows(p, s)
    arrived(1)
    total = sum_buf[0, quarter : quarter + 8]
    for i in range(1, span_count):
        total = total + sum_buf[i, quarter : quarter + 8]
    total = total / total_rows
    inner = jnp.logical_and(lane >= half, left)
    for i in range(first):
        part = total if i == 1 else pltpu.roll(total, (5 - i) % 4 * half, 1)
        b = first + i
        state_ref[8 * b : 8 * b + 8] = groups[b] + jnp.where(inner, part, 0.0)

    for copy in copies:
        copy.wait_send()
    for pair in halo:
        for copy in pair:
            copy.wait_send()

    @pl.when(mw < wall_count - 1)
    def _():
        y_up.wait_send()

    @pl.when(mw > 0)
    def _():
        y_down.wait_send()


def modes_kernel(vort, state_ref, spread_ref, out_hbm, r_hbm, out, r_ref, sem):
    snaps, comps, planes, cells, lanes = out.shape
    half = snaps // 2
    first = half // 8
    groups = [state_ref[8 * i : 8 * i + 8] for i in range(snaps // 8)]

    def blocks():
        for b in range(first):
            row = groups[b]
            yield [jnp.broadcast_to(row[k : k + 1], (8, 2 * snaps)) for k in range(8)], row
        for p, s in eliminate(groups, first, 2 * first):
            q = [p[k] / jnp.sqrt(s[k]) for k in range(8)]
            row = q[0]
            for k in range(1, 8):
                row = jnp.where(sub8 == k, q[k], row)
            yield q, row

    lane8 = lax.broadcasted_iota(jnp.int32, (8, 2 * snaps), 1)
    sub8 = lax.broadcasted_iota(jnp.int32, (8, 2 * snaps), 0)
    count = 2
    block = 8 * count
    wide = block * cells
    row_z = lax.rem(lax.broadcasted_iota(jnp.int32, (wide, snaps * cells), 0), cells)
    col_z = lax.rem(lax.broadcasted_iota(jnp.int32, (wide, snaps * cells), 1), cells)
    same = row_z == col_z
    scaled = []
    stores = []
    for b, (q, row) in enumerate(blocks()):
        row = jnp.where(lane8 < sub8 + 8 * b, 0.0, row)
        r_ref[8 * b : 8 * b + 8] = row[:, :snaps]
        scaled += q
        if b % count == count - 1:
            x = jnp.concatenate(scaled, axis=0).astype(BF)
            scaled = []
            n = b // count
            depth = (n + 1) * wide
            w = dot(x, spread_ref[:, :depth])
            w = jnp.where(same[:, :depth], w, 0.0).astype(BF)
            m = dot(w, vort[:depth])
            at = pl.ds(n * block, block)
            for comp in range(comps):
                for p_ in range(planes):
                    slab = comp * planes + p_
                    out[n * block : (n + 1) * block, comp, p_] = (
                        m[:, slab * lanes : (slab + 1) * lanes]
                        .reshape(block, cells, lanes).astype(BF)
                    )
            store = pltpu.make_async_copy(out.at[at], out_hbm.at[at], sem.at[n])
            store.start()
            stores.append(store)
    store = pltpu.make_async_copy(r_ref, r_hbm, sem.at[4])
    store.start()
    stores.append(store)
    for store in stores:
        store.wait()


def per_device(velocity, wall_metric):
    snaps, comps, depth, cells, lanes = velocity.shape
    planes = depth - 6
    spans, walls = lax.axis_size("span"), lax.axis_size("wall")
    phases, reach = 0, 1
    while 2 * reach < spans:
        phases, reach = phases + 1, 2 * reach
    total_rows = 3 * planes * cells * spans * lanes * walls
    *consts, spread = constants(snaps, cells, lanes, planes)
    vmem = pl.BlockSpec(memory_space=pltpu.VMEM)
    hbm = pl.BlockSpec(memory_space=pl.ANY)
    dma = pltpu.SemaphoreType.DMA
    half = snaps // 2
    wide = snaps * cells
    rows = half * cells
    edge = half * 3
    slabs = comps * planes
    vorticity, state = pl.pallas_call(
        functools.partial(kernel, spans, walls, total_rows),
        out_shape=(
            pltpu.VMEM((wide, slabs * lanes), BF),
            pltpu.VMEM((snaps, 2 * snaps), F32),
        ),
        in_specs=[hbm] * (2 + len(consts)),
        out_specs=(vmem, vmem),
        scratch_shapes=[
            pltpu.VMEM((1, lanes), F32),
            *[pltpu.VMEM(a.shape, a.dtype) for a in consts],
            pltpu.VMEM((snaps, planes, cells, lanes), BF),
            pltpu.VMEM((snaps, depth, cells, lanes), BF),
            pltpu.VMEM((snaps, depth, cells, lanes), BF),
            pltpu.VMEM((3, planes, rows, 2 * lanes), BF),
            pltpu.VMEM((2, planes, 2 * edge, 2 * lanes), BF),
            pltpu.VMEM((2, planes, 2 * edge, 2 * lanes), BF),
            pltpu.VMEM((rows, lanes), BF),
            pltpu.VMEM((rows, lanes), BF),
            pltpu.VMEM((rows, lanes), BF),
            pltpu.VMEM((3, planes, wide, lanes), F32),
            pltpu.VMEM((2, wide, lanes), F32),
            pltpu.VMEM((walls, half // 2 + 8, 2 * snaps), F32),
            pltpu.VMEM((spans, half // 2 + 8, 2 * snaps), F32),
            dma((12,)),
            dma((2, planes, 2)),
            dma((2, planes, 2)),
            dma((2,)),
            dma((2,)),
            dma((walls,)),
            dma((walls,)),
            dma((2, spans)),
            dma((2, spans)),
            pltpu.SemaphoreType.REGULAR((phases,)),
        ],
        compiler_params=pltpu.CompilerParams(
            collective_id=0, has_side_effects=True, vmem_limit_bytes=60 << 20
        ),
        name="pod",
    )(velocity, wall_metric.reshape(1, lanes), *consts)
    return pl.pallas_call(
        modes_kernel,
        out_shape=(
            jax.ShapeDtypeStruct((snaps, comps, planes, cells, lanes), BF),
            jax.ShapeDtypeStruct((snaps, snaps), F32),
        ),
        in_specs=[vmem, vmem, vmem],
        out_specs=(hbm, hbm),
        scratch_shapes=[
            pltpu.VMEM((snaps, comps, planes, cells, lanes), BF),
            pltpu.VMEM((snaps, snaps), F32),
            dma((5,)),
        ],
        compiler_params=pltpu.CompilerParams(vmem_limit_bytes=32 << 20),
        name="modes",
    )(vorticity, state, spread)


def solution(mesh):
    in_specs = (P(None, None, None, "span", "wall"), P("wall"))
    out_specs = (P(None, None, None, "span", "wall"), P())
    return jax.shard_map(
        per_device, mesh=mesh, in_specs=in_specs, out_specs=out_specs, check_vma=False
    )
```

```python
import functools

import jax
import jax.numpy as jnp
import ml_dtypes
import numpy as np
from jax import lax
from jax.experimental import pallas as pl
from jax.experimental.pallas import tpu as pltpu
from jax.sharding import PartitionSpec as P

MESH = pl.DeviceIdType.MESH
BF = jnp.bfloat16
F32 = jnp.float32


def coef(offset):
    table = {1: 45.0, 2: -9.0, 3: 1.0}
    size = np.abs(offset)
    out = np.zeros(offset.shape, np.float32)
    for step, value in table.items():
        out = np.where(size == step, value * np.sign(offset), out)
    return out


def constants(snaps, cells, lanes, planes):
    half = snaps // 2
    z = np.arange(cells)
    r = np.arange(3)
    eye = np.eye(half, dtype=np.float32)
    pick = np.concatenate(
        [
            np.kron(eye, (z[None, :] == r[:, None]).astype(np.float32)),
            np.kron(eye, (z[None, :] == cells - 3 + r[:, None]).astype(np.float32)),
        ],
        axis=0,
    )
    inside = np.kron(eye, coef(z[None, :] - z[:, None]))
    outside = np.concatenate(
        [
            np.kron(eye, coef(r[None, :] - 3 - z[:, None])),
            np.kron(eye, coef(cells + r[None, :] - z[:, None])),
        ],
        axis=1,
    )
    y = np.arange(lanes)
    wall = coef(y[:, None] - y[None, :])
    packs = 4 * planes
    step = lanes // packs
    gather = np.zeros((packs, lanes, lanes), np.float32)
    scatter = np.zeros((2, lanes, packs, lanes), np.float32)
    for g in range(packs):
        for t in range(3):
            gather[g, t, g * step + t] = 1.0
            gather[g, lanes - 3 + t, g * step + 3 + t] = 1.0
            scatter[0, g * step + 3 + t, g] = coef(t - 3 - y)
            scatter[1, g * step + t, g] = coef(lanes + t - y)
    gather = gather.reshape(packs * lanes, lanes)
    scatter = scatter.reshape(2 * lanes, packs * lanes)
    tables = (pick, inside, outside, gather, wall, scatter)
    return [jnp.asarray(a.astype(ml_dtypes.bfloat16)) for a in tables]


def dot(a, b):
    return jnp.dot(a, b, preferred_element_type=F32)


def eliminate(groups, start, stop):
    count = len(groups)
    sub = lax.broadcasted_iota(jnp.int32, (8, 128), 0)

    def wide(value):
        return jnp.broadcast_to(value, (8, 128))

    for b in range(start, stop):
        at = 8 * b
        p = [wide(groups[b][k : k + 1, :]) for k in range(8)]
        s = {(k, l): wide(p[k][:, at + l : at + l + 1]) for k in range(8) for l in range(k, 8)}
        inv, f = [], {}
        for k in range(8):
            inv.append(1.0 / s[k, k])
            for l in range(k + 1, 8):
                f[k, l] = s[k, l] * inv[k]
                for m in range(l, 8):
                    s[l, m] = s[l, m] - f[k, l] * s[k, m]
        for k in range(8):
            for l in range(k + 1, 8):
                p[l] = p[l] - f[k, l] * p[k]
        scaled = [p[k] * inv[k] for k in range(8)]
        for i in range(b + 1, count):
            c = [wide(groups[i][:, at + k : at + k + 1]) for k in range(8)]
            value = groups[i]
            for k in range(8):
                for l in range(k + 1, 8):
                    c[l] = c[l] - c[k] * f[k, l]
                value = value - c[k] * scaled[k]
            groups[i] = value
        yield p, [s[k, k] for k in range(8)]


def scaled_rows(p, s):
    sub = lax.broadcasted_iota(jnp.int32, (8, 128), 0)
    row = p[0] / jnp.sqrt(s[0])
    for k in range(1, 8):
        row = jnp.where(sub == k, p[k] / jnp.sqrt(s[k]), row)
    return row


def kernel(
    span_count, wall_count, total_rows,
    vel, metric_hbm, pick_hbm, inside_hbm, outside_hbm, gather_hbm, wall_hbm, scatter_hbm,
    vort, state_ref,
    metric_ref, pick_ref, inside_ref, outside_ref, gather_ref, wall_ref, scatter_ref,
    u_buf, v_buf, w_buf, flat, send_buf, halo_buf, ysend_buf, ylo_buf, yhi_buf, acc, vz,
    piece_buf, sum_buf,
    local_sem, hs_sem, hr_sem, ys_sem, yr_sem, ps_sem, pr_sem, ss_sem, sr_sem, seen,
):
    snaps, planes = u_buf.shape[0], u_buf.shape[1]
    cells, lanes = vel.shape[3], vel.shape[4]
    half = snaps // 2
    rows = half * cells
    edge = half * 3
    me = lax.axis_index("span")
    mw = lax.axis_index("wall")

    def ring(d):
        return lax.rem(me + span_count + d, span_count)

    down, up = ring(-1), ring(1)

    def load(i, src, dst):
        copy = pltpu.make_async_copy(src, dst, local_sem.at[i])
        copy.start()
        return copy

    mid = pl.ds(3, planes)
    load_pick = load(0, pick_hbm, pick_ref)
    load_u = load(1, vel.at[:, 0, mid], u_buf)
    load_v = load(2, vel.at[:, 1, mid], v_buf.at[:, mid])
    load_rest = [
        load(3, gather_hbm, gather_ref),
        load(4, vel.at[:, 2], w_buf),
        load(5, vel.at[:, 1, pl.ds(0, 3)], v_buf.at[:, pl.ds(0, 3)]),
        load(6, vel.at[:, 1, pl.ds(3 + planes, 3)], v_buf.at[:, pl.ds(3 + planes, 3)]),
        load(7, wall_hbm, wall_ref),
        load(8, scatter_hbm, scatter_ref),
        load(9, metric_hbm, metric_ref),
        load(10, inside_hbm, inside_ref),
        load(11, outside_hbm, outside_ref),
    ]

    barrier = pltpu.get_barrier_semaphore()
    for peer in (down, up):
        pl.semaphore_signal(barrier, inc=1, device_id=(peer, mw), device_id_type=MESH)
    for d in range(1, wall_count):
        pl.semaphore_signal(
            barrier, inc=1, device_id=(me, lax.rem(mw + d, wall_count)), device_id_type=MESH
        )

    def tell(phase):
        for peer in (ring(-(1 << phase)), ring(1 << phase)):
            pl.semaphore_signal(seen.at[phase], inc=1, device_id=(peer, mw), device_id_type=MESH)

    def hear(phase):
        pl.semaphore_wait(seen.at[phase], 2)

    def rows_of(value):
        return value.astype(F32).reshape(rows, lanes).astype(BF)

    def wide(buf, p):
        return jnp.concatenate(
            [rows_of(buf[k * half : (k + 1) * half, p]) for k in range(2)], axis=1
        )

    odd = lax.rem(me, 2)

    def piece(c, p, turn):
        side = 1 - odd if turn == 0 else odd
        here = pl.multiple_of(side * edge, edge)
        there = pl.multiple_of((1 - side) * edge, edge)
        return pltpu.make_async_remote_copy(
            send_buf.at[c, p, pl.ds(here, edge)], halo_buf.at[c, p, pl.ds(there, edge)],
            hs_sem.at[c, p, side], hr_sem.at[c, p, side],
            device_id=(ring(2 * side - 1), mw), device_id_type=MESH,
        )

    halo = []
    for c in range(2):
        if c == 0:
            load_pick.wait()
            load_u.wait()
        else:
            load_v.wait()
        for p in range(planes):
            f = wide(u_buf, p) if c == 0 else wide(v_buf, 3 + p)
            flat[c, p] = f
            send_buf[c, p] = dot(pick_ref[...], f).astype(BF)
            if c == 0 and p == 0:
                pl.semaphore_wait(barrier, 2 + wall_count - 1)
            halo.append([piece(c, p, turn) for turn in range(2)])
            halo[-1][0].start()
    for pair in halo:
        pair[1].start()

    phases = seen.shape[0]
    tell(0)
    for copy in load_rest:
        copy.wait()
    for p in range(planes):
        flat[2, p] = wide(w_buf, 3 + p)
    ysend_buf[...] = dot(
        jnp.concatenate([flat[2 * c, p] for c in range(2) for p in range(planes)], axis=1),
        gather_ref[...],
    ).astype(BF)

    y_up = pltpu.make_async_remote_copy(
        ysend_buf, ylo_buf, ys_sem.at[0], yr_sem.at[0],
        device_id=(me, lax.rem(mw + 1, wall_count)), device_id_type=MESH,
    )
    y_down = pltpu.make_async_remote_copy(
        ysend_buf, yhi_buf, ys_sem.at[1], yr_sem.at[1],
        device_id=(me, lax.rem(mw + wall_count - 1, wall_count)), device_id_type=MESH,
    )

    @pl.when(mw < wall_count - 1)
    def _():
        y_up.start()

    @pl.when(mw > 0)
    def _():
        y_down.start()

    @pl.when(mw == 0)
    def _():
        ylo_buf[...] = jnp.zeros_like(ylo_buf)

    @pl.when(mw == wall_count - 1)
    def _():
        yhi_buf[...] = jnp.zeros_like(yhi_buf)

    def along_x(k, carry):
        at = pl.ds(k * 4, 4)
        out = pl.ds(pl.multiple_of(k * 4 * cells, 4 * cells), 4 * cells)
        for c, buf in enumerate((v_buf, w_buf)):
            f = [buf[at, q].astype(F32) for q in range(6 + planes)]
            for p in range(planes):
                d = (
                    45.0 * (f[p + 4] - f[p + 2]) - 9.0 * (f[p + 5] - f[p + 1])
                    + (f[p + 6] - f[p])
                ).reshape(4 * cells, lanes)
                if c == 0:
                    acc[2, p, out] = d
                else:
                    acc[1, p, out] = -d
        return carry

    lax.fori_loop(0, snaps // 4, along_x, 0)

    if phases > 0:
        hear(0)
    if phases > 1:
        tell(1)

    @pl.when(mw > 0)
    def _():
        y_up.wait_recv()

    @pl.when(mw < wall_count - 1)
    def _():
        y_down.wait_recv()

    sides = jnp.concatenate([ylo_buf[...], yhi_buf[...]], axis=1)
    metric = metric_ref[...]
    for c in range(2):
        for p in range(planes):
            for k in range(2):
                g = (c * planes + p) * 2 + k
                at = slice(k * rows, (k + 1) * rows)
                f = flat[2 * c, p, :, k * lanes : (k + 1) * lanes]
                d = dot(f, wall_ref[...])
                d = d + dot(sides, scatter_ref[:, g * lanes : (g + 1) * lanes])
                d = d * metric
                if c == 0:
                    acc[2, p, at] = acc[2, p, at] - d
                else:
                    acc[0, p, at] = d

    def finish(comp, p, k, value):
        slab = comp * planes + p
        at = slice(k * rows, (k + 1) * rows)
        v = (value * (1.0 / 60.0)).astype(BF)
        vz[slab % 2, at] = v.astype(F32)

    def gram_of(slab):
        layers = [vz[slab % 2, pl.ds(z, snaps, stride=cells), :].astype(BF) for z in range(cells)]
        for z in range(cells):
            vort[z * snaps : (z + 1) * snaps, slab * lanes : (slab + 1) * lanes] = layers[z]
        a = jnp.concatenate(layers, axis=1)
        return lax.dot_general(
            a, jnp.concatenate([a, a], axis=0), (((1,), (1,)), ((), ())),
            preferred_element_type=F32,
        )

    for p in range(planes):
        for c in range(2):
            d = dot(inside_ref[...], flat[c, p])
            for k in range(2):
                at = slice(k * rows, (k + 1) * rows)
                part = d[:, k * lanes : (k + 1) * lanes]
                if c == 0:
                    acc[1, p, at] = acc[1, p, at] + part
                else:
                    acc[0, p, at] = acc[0, p, at] - part
    g = None
    for p in range(planes):
        for k in range(2):
            finish(2, p, k, acc[2, p, k * rows : (k + 1) * rows])
        part = gram_of(2 * planes + p)
        g = part if g is None else g + part
    if phases > 1:
        hear(1)
    for phase in range(2, phases):
        tell(phase)
        if phase < phases - 1:
            hear(phase)

    for c in range(2):
        for p in range(planes):
            for copy in halo[c * planes + p]:
                copy.wait_recv()
            d = dot(outside_ref[...], halo_buf[c, p])
            for k in range(2):
                at = slice(k * rows, (k + 1) * rows)
                part = d[:, k * lanes : (k + 1) * lanes]
                if c == 0:
                    finish(1, p, k, acc[1, p, at] + part)
                else:
                    finish(0, p, k, acc[0, p, at] - part)
            g = g + gram_of((1 - c) * planes + p)
    if phases > 2:
        hear(phases - 1)

    quarter = half // 2
    lane = lax.broadcasted_iota(jnp.int32, (8, 2 * snaps), 1)
    sub = lax.broadcasted_iota(jnp.int32, (8, 2 * snaps), 0)
    left = lane < snaps
    for i in range(quarter // 8):
        at = slice(8 * i, 8 * i + 8)
        piece_buf[mw, at] = jnp.where(left, g[at], g[quarter + 8 * i : quarter + 8 * i + 8])
    corner = None
    for i in range(4):
        part = g[half + 8 * i : half + 8 * i + 8]
        if i % 2 == 0:
            part = pltpu.roll(part, half, 1)
        corner = part if corner is None else jnp.where(lane < half * i, corner, part)
    piece_buf[mw, quarter : quarter + 8] = corner
    copies = []

    def remote(src, dst, send, recv, device):
        copy = pltpu.make_async_remote_copy(
            src, dst, send, recv, device_id=device, device_id_type=MESH
        )
        copy.start()
        return copy

    started = []
    for d in range(1, wall_count):
        w = lax.rem(mw + d, wall_count)
        started.append(
            remote(piece_buf.at[mw], piece_buf.at[mw], ps_sem.at[d], pr_sem.at[d], (me, w))
        )
    for copy in started:
        copy.wait_recv()
    copies += started
    total = piece_buf[0]
    for w in range(1, wall_count):
        total = total + piece_buf[w]
    sum_buf[me] = total
    others = [i + (me <= i).astype(jnp.int32) for i in range(span_count - 1)]
    parts = (pl.ds(0, quarter + 8),)

    def to(turn, peer):
        mine = sum_buf.at[me, parts[turn]]
        copies.append(
            remote(mine, mine, ss_sem.at[turn, peer], sr_sem.at[turn, me], (peer, mw))
        )

    def arrived(turn):
        for peer in others:
            theirs = sum_buf.at[peer, parts[turn]]
            pltpu.make_async_remote_copy(
                theirs, theirs, ss_sem.at[turn, peer], sr_sem.at[turn, peer],
                device_id=(peer, mw), device_id_type=MESH,
            ).wait_recv()

    for peer in others:
        to(0, peer)
    arrived(0)
    total = sum_buf[0, 0:quarter]
    for i in range(1, span_count):
        total = total + sum_buf[i, 0:quarter]
    total = total / total_rows
    top = jnp.concatenate([total, pltpu.roll(total, snaps, 1)], axis=0)
    turned = jnp.concatenate([top] * 4, axis=0).T
    groups = []
    for i in range(snaps // 8):
        if 8 * i < half:
            value = top[8 * i : 8 * i + 8]
        else:
            value = jnp.where(lane < half, turned[8 * i : 8 * i + 8], 0.0)
        groups.append(jnp.where(left, value, (lane - snaps - 8 * i == sub).astype(F32)))
    first = half // 8
    for b, (p, s) in enumerate(eliminate(groups, 0, first)):
        state_ref[8 * b : 8 * b + 8] = scaled_rows(p, s)
    total = sum_buf[0, quarter : quarter + 8]
    for i in range(1, span_count):
        total = total + sum_buf[i, quarter : quarter + 8]
    total = total / total_rows
    inner = jnp.logical_and(lane >= half, left)
    for i in range(first):
        part = total if i == 1 else pltpu.roll(total, (5 - i) % 4 * half, 1)
        b = first + i
        state_ref[8 * b : 8 * b + 8] = groups[b] + jnp.where(inner, part, 0.0)

    for copy in copies:
        copy.wait_send()
    for pair in halo:
        for copy in pair:
            copy.wait_send()

    @pl.when(mw < wall_count - 1)
    def _():
        y_up.wait_send()

    @pl.when(mw > 0)
    def _():
        y_down.wait_send()


def modes_kernel(vort, state_ref, out_hbm, r_hbm, out, r_ref, sem):
    snaps, comps, planes, cells, lanes = out.shape
    half = snaps // 2
    first = half // 8
    groups = [state_ref[8 * i : 8 * i + 8] for i in range(snaps // 8)]

    def blocks():
        for b in range(first):
            row = groups[b]
            yield [jnp.broadcast_to(row[k : k + 1], (8, 2 * snaps)) for k in range(8)], row
        for p, s in eliminate(groups, first, 2 * first):
            q = [p[k] / jnp.sqrt(s[k]) for k in range(8)]
            row = q[0]
            for k in range(1, 8):
                row = jnp.where(sub8 == k, q[k], row)
            yield q, row

    lane8 = lax.broadcasted_iota(jnp.int32, (8, 2 * snaps), 1)
    sub8 = lax.broadcasted_iota(jnp.int32, (8, 2 * snaps), 0)
    count = 2
    block = 8 * count
    layer = lane8 // snaps
    scaled = []
    stores = []
    for b, (q, row) in enumerate(blocks()):
        row = jnp.where(lane8 < sub8 + 8 * b, 0.0, row)
        r_ref[8 * b : 8 * b + 8] = row[:, :snaps]
        for value in q:
            twice = jnp.where(lane8 < snaps, pltpu.roll(value, snaps, 1), value)
            scaled.append(
                jnp.concatenate(
                    [jnp.where(layer + 2 * v == sub8, twice, 0.0) for v in range(cells // 2)],
                    axis=1,
                )
            )
        if b % count == count - 1:
            w = jnp.concatenate(scaled, axis=0).astype(BF)
            scaled = []
            n = b // count
            m = dot(w, vort[...])
            at = pl.ds(n * block, block)
            for comp in range(comps):
                for p_ in range(planes):
                    slab = comp * planes + p_
                    out[n * block : (n + 1) * block, comp, p_] = (
                        m[:, slab * lanes : (slab + 1) * lanes]
                        .reshape(block, cells, lanes).astype(BF)
                    )
            store = pltpu.make_async_copy(out.at[at], out_hbm.at[at], sem.at[n])
            store.start()
            stores.append(store)
    store = pltpu.make_async_copy(r_ref, r_hbm, sem.at[4])
    store.start()
    stores.append(store)
    for store in stores:
        store.wait()


def per_device(velocity, wall_metric):
    snaps, comps, depth, cells, lanes = velocity.shape
    planes = depth - 6
    spans, walls = lax.axis_size("span"), lax.axis_size("wall")
    phases, reach = 0, 1
    while 2 * reach < spans:
        phases, reach = phases + 1, 2 * reach
    total_rows = 3 * planes * cells * spans * lanes * walls
    consts = constants(snaps, cells, lanes, planes)
    vmem = pl.BlockSpec(memory_space=pltpu.VMEM)
    hbm = pl.BlockSpec(memory_space=pl.ANY)
    dma = pltpu.SemaphoreType.DMA
    half = snaps // 2
    wide = snaps * cells
    rows = half * cells
    edge = half * 3
    slabs = comps * planes
    vorticity, state = pl.pallas_call(
        functools.partial(kernel, spans, walls, total_rows),
        out_shape=(
            pltpu.VMEM((wide, slabs * lanes), BF),
            pltpu.VMEM((snaps, 2 * snaps), F32),
        ),
        in_specs=[hbm] * (2 + len(consts)),
        out_specs=(vmem, vmem),
        scratch_shapes=[
            pltpu.VMEM((1, lanes), F32),
            *[pltpu.VMEM(a.shape, a.dtype) for a in consts],
            pltpu.VMEM((snaps, planes, cells, lanes), BF),
            pltpu.VMEM((snaps, depth, cells, lanes), BF),
            pltpu.VMEM((snaps, depth, cells, lanes), BF),
            pltpu.VMEM((3, planes, rows, 2 * lanes), BF),
            pltpu.VMEM((2, planes, 2 * edge, 2 * lanes), BF),
            pltpu.VMEM((2, planes, 2 * edge, 2 * lanes), BF),
            pltpu.VMEM((rows, lanes), BF),
            pltpu.VMEM((rows, lanes), BF),
            pltpu.VMEM((rows, lanes), BF),
            pltpu.VMEM((3, planes, wide, lanes), F32),
            pltpu.VMEM((2, wide, lanes), F32),
            pltpu.VMEM((walls, half // 2 + 8, 2 * snaps), F32),
            pltpu.VMEM((spans, half // 2 + 8, 2 * snaps), F32),
            dma((12,)),
            dma((2, planes, 2)),
            dma((2, planes, 2)),
            dma((2,)),
            dma((2,)),
            dma((walls,)),
            dma((walls,)),
            dma((2, spans)),
            dma((2, spans)),
            pltpu.SemaphoreType.REGULAR((phases,)),
        ],
        compiler_params=pltpu.CompilerParams(
            collective_id=0, has_side_effects=True, vmem_limit_bytes=60 << 20
        ),
        name="pod",
    )(velocity, wall_metric.reshape(1, lanes), *consts)
    return pl.pallas_call(
        modes_kernel,
        out_shape=(
            jax.ShapeDtypeStruct((snaps, comps, planes, cells, lanes), BF),
            jax.ShapeDtypeStruct((snaps, snaps), F32),
        ),
        in_specs=[vmem, vmem],
        out_specs=(hbm, hbm),
        scratch_shapes=[
            pltpu.VMEM((snaps, comps, planes, cells, lanes), BF),
            pltpu.VMEM((snaps, snaps), F32),
            dma((5,)),
        ],
        compiler_params=pltpu.CompilerParams(vmem_limit_bytes=32 << 20),
        name="modes",
    )(vorticity, state)


def solution(mesh):
    in_specs = (P(None, None, None, "span", "wall"), P("wall"))
    out_specs = (P(None, None, None, "span", "wall"), P())
    return jax.shard_map(
        per_device, mesh=mesh, in_specs=in_specs, out_specs=out_specs, check_vma=False
    )
```

```python
import functools

import jax
import jax.numpy as jnp
import ml_dtypes
import numpy as np
from jax import lax
from jax.experimental import pallas as pl
from jax.experimental.pallas import tpu as pltpu
from jax.sharding import PartitionSpec as P

MESH = pl.DeviceIdType.MESH
BF = jnp.bfloat16
F32 = jnp.float32


def coef(offset):
    table = {1: 45.0, 2: -9.0, 3: 1.0}
    size = np.abs(offset)
    out = np.zeros(offset.shape, np.float32)
    for step, value in table.items():
        out = np.where(size == step, value * np.sign(offset), out)
    return out


def constants(snaps, cells, lanes, planes):
    half = snaps // 2
    z = np.arange(cells)
    r = np.arange(3)
    eye = np.eye(half, dtype=np.float32)
    pick = np.concatenate(
        [
            np.kron(eye, (z[None, :] == r[:, None]).astype(np.float32)),
            np.kron(eye, (z[None, :] == cells - 3 + r[:, None]).astype(np.float32)),
        ],
        axis=0,
    )
    inside = np.kron(eye, coef(z[None, :] - z[:, None]))
    outside = np.concatenate(
        [
            np.kron(eye, coef(r[None, :] - 3 - z[:, None])),
            np.kron(eye, coef(cells + r[None, :] - z[:, None])),
        ],
        axis=1,
    )
    y = np.arange(lanes)
    wall = coef(y[:, None] - y[None, :])
    packs = 4 * planes
    step = lanes // packs
    gather = np.zeros((packs, lanes, lanes), np.float32)
    scatter = np.zeros((2, lanes, packs, lanes), np.float32)
    for g in range(packs):
        for t in range(3):
            gather[g, t, g * step + t] = 1.0
            gather[g, lanes - 3 + t, g * step + 3 + t] = 1.0
            scatter[0, g * step + 3 + t, g] = coef(t - 3 - y)
            scatter[1, g * step + t, g] = coef(lanes + t - y)
    gather = gather.reshape(packs * lanes, lanes)
    scatter = scatter.reshape(2 * lanes, packs * lanes)
    tables = (pick, inside, outside, gather, wall, scatter)
    return [jnp.asarray(a.astype(ml_dtypes.bfloat16)) for a in tables]


def dot(a, b):
    return jnp.dot(a, b, preferred_element_type=F32)


def eliminate(groups, start, stop):
    count = len(groups)
    sub = lax.broadcasted_iota(jnp.int32, (8, 128), 0)

    def wide(value):
        return jnp.broadcast_to(value, (8, 128))

    for b in range(start, stop):
        at = 8 * b
        p = [wide(groups[b][k : k + 1, :]) for k in range(8)]
        s = {(k, l): wide(p[k][:, at + l : at + l + 1]) for k in range(8) for l in range(k, 8)}
        inv, f = [], {}
        for k in range(8):
            inv.append(1.0 / s[k, k])
            for l in range(k + 1, 8):
                f[k, l] = s[k, l] * inv[k]
                for m in range(l, 8):
                    s[l, m] = s[l, m] - f[k, l] * s[k, m]
        for k in range(8):
            for l in range(k + 1, 8):
                p[l] = p[l] - f[k, l] * p[k]
        scaled = [p[k] * inv[k] for k in range(8)]
        for i in range(b + 1, count):
            c = [wide(groups[i][:, at + k : at + k + 1]) for k in range(8)]
            value = groups[i]
            for k in range(8):
                for l in range(k + 1, 8):
                    c[l] = c[l] - c[k] * f[k, l]
                value = value - c[k] * scaled[k]
            groups[i] = value
        yield p, [s[k, k] for k in range(8)]


def scaled_rows(p, s):
    sub = lax.broadcasted_iota(jnp.int32, (8, 128), 0)
    row = p[0] / jnp.sqrt(s[0])
    for k in range(1, 8):
        row = jnp.where(sub == k, p[k] / jnp.sqrt(s[k]), row)
    return row


def kernel(
    span_count, wall_count, total_rows,
    vel, metric_hbm, pick_hbm, inside_hbm, outside_hbm, gather_hbm, wall_hbm, scatter_hbm,
    vort, state_ref,
    metric_ref, pick_ref, inside_ref, outside_ref, gather_ref, wall_ref, scatter_ref,
    u_buf, v_buf, w_buf, flat, send_buf, halo_buf, ysend_buf, ylo_buf, yhi_buf, acc, vz,
    piece_buf, sum_buf, corner_buf, full_buf,
    local_sem, hs_sem, hr_sem, ys_sem, yr_sem, ps_sem, pr_sem, ss_sem, sr_sem, fs_sem, fr_sem, seen,
):
    snaps, planes = u_buf.shape[0], u_buf.shape[1]
    cells, lanes = vel.shape[3], vel.shape[4]
    half = snaps // 2
    rows = half * cells
    edge = half * 3
    me = lax.axis_index("span")
    mw = lax.axis_index("wall")

    def ring(d):
        return lax.rem(me + span_count + d, span_count)

    down, up = ring(-1), ring(1)

    def load(i, src, dst):
        copy = pltpu.make_async_copy(src, dst, local_sem.at[i])
        copy.start()
        return copy

    mid = pl.ds(3, planes)
    load_pick = load(0, pick_hbm, pick_ref)
    load_u = load(1, vel.at[:, 0, mid], u_buf)
    load_v = load(2, vel.at[:, 1, mid], v_buf.at[:, mid])
    load_rest = [
        load(3, gather_hbm, gather_ref),
        load(4, vel.at[:, 2], w_buf),
        load(5, vel.at[:, 1, pl.ds(0, 3)], v_buf.at[:, pl.ds(0, 3)]),
        load(6, vel.at[:, 1, pl.ds(3 + planes, 3)], v_buf.at[:, pl.ds(3 + planes, 3)]),
        load(7, wall_hbm, wall_ref),
        load(8, scatter_hbm, scatter_ref),
        load(9, metric_hbm, metric_ref),
        load(10, inside_hbm, inside_ref),
        load(11, outside_hbm, outside_ref),
    ]

    barrier = pltpu.get_barrier_semaphore()
    for peer in (down, up):
        pl.semaphore_signal(barrier, inc=1, device_id=(peer, mw), device_id_type=MESH)
    for d in range(1, wall_count):
        pl.semaphore_signal(
            barrier, inc=1, device_id=(me, lax.rem(mw + d, wall_count)), device_id_type=MESH
        )

    def tell(phase):
        for peer in (ring(-(1 << phase)), ring(1 << phase)):
            pl.semaphore_signal(seen.at[phase], inc=1, device_id=(peer, mw), device_id_type=MESH)

    def hear(phase):
        pl.semaphore_wait(seen.at[phase], 2)

    def rows_of(value):
        return value.astype(F32).reshape(rows, lanes).astype(BF)

    def wide(buf, p):
        return jnp.concatenate(
            [rows_of(buf[k * half : (k + 1) * half, p]) for k in range(2)], axis=1
        )

    odd = lax.rem(me, 2)

    def piece(c, p, turn):
        side = 1 - odd if turn == 0 else odd
        here = pl.multiple_of(side * edge, edge)
        there = pl.multiple_of((1 - side) * edge, edge)
        return pltpu.make_async_remote_copy(
            send_buf.at[c, p, pl.ds(here, edge)], halo_buf.at[c, p, pl.ds(there, edge)],
            hs_sem.at[c, p, side], hr_sem.at[c, p, side],
            device_id=(ring(2 * side - 1), mw), device_id_type=MESH,
        )

    halo = []
    for c in range(2):
        if c == 0:
            load_pick.wait()
            load_u.wait()
        else:
            load_v.wait()
        for p in range(planes):
            f = wide(u_buf, p) if c == 0 else wide(v_buf, 3 + p)
            flat[c, p] = f
            send_buf[c, p] = dot(pick_ref[...], f).astype(BF)
            if c == 0 and p == 0:
                pl.semaphore_wait(barrier, 2 + wall_count - 1)
            halo.append([piece(c, p, turn) for turn in range(2)])
            halo[-1][0].start()
    for pair in halo:
        pair[1].start()

    phases = seen.shape[0]
    tell(0)
    for copy in load_rest:
        copy.wait()
    for p in range(planes):
        flat[2, p] = wide(w_buf, 3 + p)
    ysend_buf[...] = dot(
        jnp.concatenate([flat[2 * c, p] for c in range(2) for p in range(planes)], axis=1),
        gather_ref[...],
    ).astype(BF)

    y_up = pltpu.make_async_remote_copy(
        ysend_buf, ylo_buf, ys_sem.at[0], yr_sem.at[0],
        device_id=(me, lax.rem(mw + 1, wall_count)), device_id_type=MESH,
    )
    y_down = pltpu.make_async_remote_copy(
        ysend_buf, yhi_buf, ys_sem.at[1], yr_sem.at[1],
        device_id=(me, lax.rem(mw + wall_count - 1, wall_count)), device_id_type=MESH,
    )

    @pl.when(mw < wall_count - 1)
    def _():
        y_up.start()

    @pl.when(mw > 0)
    def _():
        y_down.start()

    @pl.when(mw == 0)
    def _():
        ylo_buf[...] = jnp.zeros_like(ylo_buf)

    @pl.when(mw == wall_count - 1)
    def _():
        yhi_buf[...] = jnp.zeros_like(yhi_buf)

    def along_x(k, carry):
        at = pl.ds(k * 4, 4)
        out = pl.ds(pl.multiple_of(k * 4 * cells, 4 * cells), 4 * cells)
        for c, buf in enumerate((v_buf, w_buf)):
            f = [buf[at, q].astype(F32) for q in range(6 + planes)]
            for p in range(planes):
                d = (
                    45.0 * (f[p + 4] - f[p + 2]) - 9.0 * (f[p + 5] - f[p + 1])
                    + (f[p + 6] - f[p])
                ).reshape(4 * cells, lanes)
                if c == 0:
                    acc[2, p, out] = d
                else:
                    acc[1, p, out] = -d
        return carry

    lax.fori_loop(0, snaps // 4, along_x, 0)

    if phases > 0:
        hear(0)
    if phases > 1:
        tell(1)

    @pl.when(mw > 0)
    def _():
        y_up.wait_recv()

    @pl.when(mw < wall_count - 1)
    def _():
        y_down.wait_recv()

    sides = jnp.concatenate([ylo_buf[...], yhi_buf[...]], axis=1)
    metric = metric_ref[...]
    for c in range(2):
        for p in range(planes):
            for k in range(2):
                g = (c * planes + p) * 2 + k
                at = slice(k * rows, (k + 1) * rows)
                f = flat[2 * c, p, :, k * lanes : (k + 1) * lanes]
                d = dot(f, wall_ref[...])
                d = d + dot(sides, scatter_ref[:, g * lanes : (g + 1) * lanes])
                d = d * metric
                if c == 0:
                    acc[2, p, at] = acc[2, p, at] - d
                else:
                    acc[0, p, at] = d

    def finish(comp, p, k, value):
        slab = comp * planes + p
        at = slice(k * rows, (k + 1) * rows)
        v = (value * (1.0 / 60.0)).astype(BF)
        vz[slab % 2, at] = v.astype(F32)

    def gram_of(slab):
        layers = [vz[slab % 2, pl.ds(z, snaps, stride=cells), :].astype(BF) for z in range(cells)]
        for z in range(cells):
            vort[z * snaps : (z + 1) * snaps, slab * lanes : (slab + 1) * lanes] = layers[z]
        a = jnp.concatenate(layers, axis=1)
        return lax.dot_general(
            a, jnp.concatenate([a, a], axis=0), (((1,), (1,)), ((), ())),
            preferred_element_type=F32,
        )

    for p in range(planes):
        for c in range(2):
            d = dot(inside_ref[...], flat[c, p])
            for k in range(2):
                at = slice(k * rows, (k + 1) * rows)
                part = d[:, k * lanes : (k + 1) * lanes]
                if c == 0:
                    acc[1, p, at] = acc[1, p, at] + part
                else:
                    acc[0, p, at] = acc[0, p, at] - part
    g = None
    for p in range(planes):
        for k in range(2):
            finish(2, p, k, acc[2, p, k * rows : (k + 1) * rows])
        part = gram_of(2 * planes + p)
        g = part if g is None else g + part
    if phases > 1:
        hear(1)
    for phase in range(2, phases):
        tell(phase)
        if phase < phases - 1:
            hear(phase)

    for c in range(2):
        for p in range(planes):
            for copy in halo[c * planes + p]:
                copy.wait_recv()
            d = dot(outside_ref[...], halo_buf[c, p])
            for k in range(2):
                at = slice(k * rows, (k + 1) * rows)
                part = d[:, k * lanes : (k + 1) * lanes]
                if c == 0:
                    finish(1, p, k, acc[1, p, at] + part)
                else:
                    finish(0, p, k, acc[0, p, at] - part)
            g = g + gram_of((1 - c) * planes + p)
    if phases > 2:
        hear(phases - 1)

    quarter = half // 2
    lane = lax.broadcasted_iota(jnp.int32, (8, 2 * snaps), 1)
    sub = lax.broadcasted_iota(jnp.int32, (8, 2 * snaps), 0)
    left = lane < snaps
    for i in range(quarter // 8):
        at = slice(8 * i, 8 * i + 8)
        piece_buf[mw, at] = jnp.where(left, g[at], g[quarter + 8 * i : quarter + 8 * i + 8])
    corner = None
    for i in range(4):
        part = g[half + 8 * i : half + 8 * i + 8]
        if i % 2 == 0:
            part = pltpu.roll(part, half, 1)
        corner = part if corner is None else jnp.where(lane < half * i, corner, part)
    piece_buf[mw, quarter : quarter + 8] = corner
    copies = []

    def remote(src, dst, send, recv, device):
        copy = pltpu.make_async_remote_copy(
            src, dst, send, recv, device_id=device, device_id_type=MESH
        )
        copy.start()
        return copy

    started = []
    for d in range(1, wall_count):
        w = lax.rem(mw + d, wall_count)
        started.append(
            remote(piece_buf.at[mw], piece_buf.at[mw], ps_sem.at[d], pr_sem.at[d], (me, w))
        )
    for copy in started:
        copy.wait_recv()
    copies += started
    total = piece_buf[0]
    for w in range(1, wall_count):
        total = total + piece_buf[w]
    low = 8 // wall_count
    corner_buf[...] = total[quarter : quarter + 8]
    sum_buf[me, 0:quarter] = total[:quarter]
    sum_buf[me, quarter : quarter + low] = corner_buf[pl.ds(mw * low, low)]
    others = [i + (me <= i).astype(jnp.int32) for i in range(span_count - 1)]
    parts = (pl.ds(0, quarter + low),)

    def to(turn, peer):
        mine = sum_buf.at[me, parts[turn]]
        copies.append(
            remote(mine, mine, ss_sem.at[turn, peer], sr_sem.at[turn, me], (peer, mw))
        )

    def arrived(turn):
        for peer in others:
            theirs = sum_buf.at[peer, parts[turn]]
            pltpu.make_async_remote_copy(
                theirs, theirs, ss_sem.at[turn, peer], sr_sem.at[turn, peer],
                device_id=(peer, mw), device_id_type=MESH,
            ).wait_recv()

    for peer in others:
        to(0, peer)
    arrived(0)
    total = sum_buf[0]
    for i in range(1, span_count):
        total = total + sum_buf[i]
    total = total / total_rows
    full_buf[mw] = total[quarter:]
    started = []
    for d in range(1, wall_count):
        w = lax.rem(mw + d, wall_count)
        started.append(
            remote(full_buf.at[mw], full_buf.at[mw], fs_sem.at[d], fr_sem.at[d], (me, w))
        )
    total = total[:quarter]
    top = jnp.concatenate([total, pltpu.roll(total, snaps, 1)], axis=0)
    turned = jnp.concatenate([top] * 4, axis=0).T
    groups = []
    for i in range(snaps // 8):
        if 8 * i < half:
            value = top[8 * i : 8 * i + 8]
        else:
            value = jnp.where(lane < half, turned[8 * i : 8 * i + 8], 0.0)
        groups.append(jnp.where(left, value, (lane - snaps - 8 * i == sub).astype(F32)))
    first = half // 8
    for b, (p, s) in enumerate(eliminate(groups, 0, first)):
        state_ref[8 * b : 8 * b + 8] = scaled_rows(p, s)
    for copy in started:
        copy.wait_recv()
    copies += started
    for w in range(wall_count):
        corner_buf[w * low : (w + 1) * low] = full_buf[w]
    total = corner_buf[...]
    inner = jnp.logical_and(lane >= half, left)
    for i in range(first):
        part = total if i == 1 else pltpu.roll(total, (5 - i) % 4 * half, 1)
        b = first + i
        state_ref[8 * b : 8 * b + 8] = groups[b] + jnp.where(inner, part, 0.0)

    for copy in copies:
        copy.wait_send()
    for pair in halo:
        for copy in pair:
            copy.wait_send()

    @pl.when(mw < wall_count - 1)
    def _():
        y_up.wait_send()

    @pl.when(mw > 0)
    def _():
        y_down.wait_send()


def modes_kernel(vort, state_ref, out_hbm, r_hbm, out, r_ref, sem):
    snaps, comps, planes, cells, lanes = out.shape
    half = snaps // 2
    first = half // 8
    groups = [state_ref[8 * i : 8 * i + 8] for i in range(snaps // 8)]

    def blocks():
        for b in range(first):
            row = groups[b]
            yield [jnp.broadcast_to(row[k : k + 1], (8, 2 * snaps)) for k in range(8)], row
        for p, s in eliminate(groups, first, 2 * first):
            q = [p[k] / jnp.sqrt(s[k]) for k in range(8)]
            row = q[0]
            for k in range(1, 8):
                row = jnp.where(sub8 == k, q[k], row)
            yield q, row

    lane8 = lax.broadcasted_iota(jnp.int32, (8, 2 * snaps), 1)
    sub8 = lax.broadcasted_iota(jnp.int32, (8, 2 * snaps), 0)
    count = 2
    block = 8 * count
    layer = lane8 // snaps
    scaled = []
    stores = []
    for b, (q, row) in enumerate(blocks()):
        row = jnp.where(lane8 < sub8 + 8 * b, 0.0, row)
        r_ref[8 * b : 8 * b + 8] = row[:, :snaps]
        for value in q:
            twice = jnp.where(lane8 < snaps, pltpu.roll(value, snaps, 1), value)
            scaled.append(
                jnp.concatenate(
                    [jnp.where(layer + 2 * v == sub8, twice, 0.0) for v in range(cells // 2)],
                    axis=1,
                )
            )
        if b % count == count - 1:
            w = jnp.concatenate(scaled, axis=0).astype(BF)
            scaled = []
            n = b // count
            m = dot(w, vort[...])
            at = pl.ds(n * block, block)
            for comp in range(comps):
                for p_ in range(planes):
                    slab = comp * planes + p_
                    out[n * block : (n + 1) * block, comp, p_] = (
                        m[:, slab * lanes : (slab + 1) * lanes]
                        .reshape(block, cells, lanes).astype(BF)
                    )
            store = pltpu.make_async_copy(out.at[at], out_hbm.at[at], sem.at[n])
            store.start()
            stores.append(store)
    store = pltpu.make_async_copy(r_ref, r_hbm, sem.at[4])
    store.start()
    stores.append(store)
    for store in stores:
        store.wait()


def per_device(velocity, wall_metric):
    snaps, comps, depth, cells, lanes = velocity.shape
    planes = depth - 6
    spans, walls = lax.axis_size("span"), lax.axis_size("wall")
    phases, reach = 0, 1
    while 2 * reach < spans:
        phases, reach = phases + 1, 2 * reach
    total_rows = 3 * planes * cells * spans * lanes * walls
    consts = constants(snaps, cells, lanes, planes)
    vmem = pl.BlockSpec(memory_space=pltpu.VMEM)
    hbm = pl.BlockSpec(memory_space=pl.ANY)
    dma = pltpu.SemaphoreType.DMA
    half = snaps // 2
    wide = snaps * cells
    rows = half * cells
    edge = half * 3
    slabs = comps * planes
    vorticity, state = pl.pallas_call(
        functools.partial(kernel, spans, walls, total_rows),
        out_shape=(
            pltpu.VMEM((wide, slabs * lanes), BF),
            pltpu.VMEM((snaps, 2 * snaps), F32),
        ),
        in_specs=[hbm] * (2 + len(consts)),
        out_specs=(vmem, vmem),
        scratch_shapes=[
            pltpu.VMEM((1, lanes), F32),
            *[pltpu.VMEM(a.shape, a.dtype) for a in consts],
            pltpu.VMEM((snaps, planes, cells, lanes), BF),
            pltpu.VMEM((snaps, depth, cells, lanes), BF),
            pltpu.VMEM((snaps, depth, cells, lanes), BF),
            pltpu.VMEM((3, planes, rows, 2 * lanes), BF),
            pltpu.VMEM((2, planes, 2 * edge, 2 * lanes), BF),
            pltpu.VMEM((2, planes, 2 * edge, 2 * lanes), BF),
            pltpu.VMEM((rows, lanes), BF),
            pltpu.VMEM((rows, lanes), BF),
            pltpu.VMEM((rows, lanes), BF),
            pltpu.VMEM((3, planes, wide, lanes), F32),
            pltpu.VMEM((2, wide, lanes), F32),
            pltpu.VMEM((walls, half // 2 + 8, 2 * snaps), F32),
            pltpu.VMEM((spans, half // 2 + 8 // walls, 2 * snaps), F32),
            pltpu.VMEM((8, 2 * snaps), F32),
            pltpu.VMEM((walls, 8 // walls, 2 * snaps), F32),
            dma((12,)),
            dma((2, planes, 2)),
            dma((2, planes, 2)),
            dma((2,)),
            dma((2,)),
            dma((walls,)),
            dma((walls,)),
            dma((1, spans)),
            dma((1, spans)),
            dma((walls,)),
            dma((walls,)),
            pltpu.SemaphoreType.REGULAR((phases,)),
        ],
        compiler_params=pltpu.CompilerParams(
            collective_id=0, has_side_effects=True, vmem_limit_bytes=60 << 20
        ),
        name="pod",
    )(velocity, wall_metric.reshape(1, lanes), *consts)
    return pl.pallas_call(
        modes_kernel,
        out_shape=(
            jax.ShapeDtypeStruct((snaps, comps, planes, cells, lanes), BF),
            jax.ShapeDtypeStruct((snaps, snaps), F32),
        ),
        in_specs=[vmem, vmem],
        out_specs=(hbm, hbm),
        scratch_shapes=[
            pltpu.VMEM((snaps, comps, planes, cells, lanes), BF),
            pltpu.VMEM((snaps, snaps), F32),
            dma((5,)),
        ],
        compiler_params=pltpu.CompilerParams(vmem_limit_bytes=32 << 20),
        name="modes",
    )(vorticity, state)


def solution(mesh):
    in_specs = (P(None, None, None, "span", "wall"), P("wall"))
    out_specs = (P(None, None, None, "span", "wall"), P())
    return jax.shard_map(
        per_device, mesh=mesh, in_specs=in_specs, out_specs=out_specs, check_vma=False
    )
```

```python
import functools

import jax
import jax.numpy as jnp
import ml_dtypes
import numpy as np
from jax import lax
from jax.experimental import pallas as pl
from jax.experimental.pallas import tpu as pltpu
from jax.sharding import PartitionSpec as P

MESH = pl.DeviceIdType.MESH
BF = jnp.bfloat16
F32 = jnp.float32


def coef(offset):
    table = {1: 45.0, 2: -9.0, 3: 1.0}
    size = np.abs(offset)
    out = np.zeros(offset.shape, np.float32)
    for step, value in table.items():
        out = np.where(size == step, value * np.sign(offset), out)
    return out


def constants(snaps, cells, lanes, planes):
    half = snaps // 2
    z = np.arange(cells)
    r = np.arange(3)
    eye = np.eye(half, dtype=np.float32)
    pick = np.concatenate(
        [
            np.kron(eye, (z[None, :] == r[:, None]).astype(np.float32)),
            np.kron(eye, (z[None, :] == cells - 3 + r[:, None]).astype(np.float32)),
        ],
        axis=0,
    )
    inside = np.kron(eye, coef(z[None, :] - z[:, None]))
    outside = np.concatenate(
        [
            np.kron(eye, coef(r[None, :] - 3 - z[:, None])),
            np.kron(eye, coef(cells + r[None, :] - z[:, None])),
        ],
        axis=1,
    )
    y = np.arange(lanes)
    wall = coef(y[:, None] - y[None, :])
    packs = 4 * planes
    step = lanes // packs
    gather = np.zeros((packs, lanes, lanes), np.float32)
    scatter = np.zeros((2, lanes, packs, lanes), np.float32)
    for g in range(packs):
        for t in range(3):
            gather[g, t, g * step + t] = 1.0
            gather[g, lanes - 3 + t, g * step + 3 + t] = 1.0
            scatter[0, g * step + 3 + t, g] = coef(t - 3 - y)
            scatter[1, g * step + t, g] = coef(lanes + t - y)
    gather = gather.reshape(packs * lanes, lanes)
    scatter = scatter.reshape(2 * lanes, packs * lanes)
    tables = (pick, inside, outside, gather, wall, scatter)
    return [jnp.asarray(a.astype(ml_dtypes.bfloat16)) for a in tables]


def dot(a, b):
    return jnp.dot(a, b, preferred_element_type=F32)


def eliminate(groups, start, stop):
    count = len(groups)
    sub = lax.broadcasted_iota(jnp.int32, (8, 128), 0)

    def wide(value):
        return jnp.broadcast_to(value, (8, 128))

    for b in range(start, stop):
        at = 8 * b
        p = [wide(groups[b][k : k + 1, :]) for k in range(8)]
        s = {(k, l): wide(p[k][:, at + l : at + l + 1]) for k in range(8) for l in range(k, 8)}
        inv, f = [], {}
        for k in range(8):
            inv.append(1.0 / s[k, k])
            for l in range(k + 1, 8):
                f[k, l] = s[k, l] * inv[k]
                for m in range(l, 8):
                    s[l, m] = s[l, m] - f[k, l] * s[k, m]
        for k in range(8):
            for l in range(k + 1, 8):
                p[l] = p[l] - f[k, l] * p[k]
        scaled = [p[k] * inv[k] for k in range(8)]
        for i in range(b + 1, count):
            c = [wide(groups[i][:, at + k : at + k + 1]) for k in range(8)]
            value = groups[i]
            for k in range(8):
                for l in range(k + 1, 8):
                    c[l] = c[l] - c[k] * f[k, l]
                value = value - c[k] * scaled[k]
            groups[i] = value
        yield p, [s[k, k] for k in range(8)]


def scaled_rows(p, s):
    sub = lax.broadcasted_iota(jnp.int32, (8, 128), 0)
    row = p[0] / jnp.sqrt(s[0])
    for k in range(1, 8):
        row = jnp.where(sub == k, p[k] / jnp.sqrt(s[k]), row)
    return row


def kernel(
    span_count, wall_count, total_rows,
    vel, metric_hbm, pick_hbm, inside_hbm, outside_hbm, gather_hbm, wall_hbm, scatter_hbm,
    vort, state_ref,
    metric_ref, pick_ref, inside_ref, outside_ref, gather_ref, wall_ref, scatter_ref,
    u_buf, v_buf, w_buf, flat, send_buf, halo_buf, ysend_buf, ylo_buf, yhi_buf, acc, vz,
    piece_buf, sum_buf, corner_buf, full_buf,
    local_sem, hs_sem, hr_sem, ys_sem, yr_sem, ps_sem, pr_sem, ss_sem, sr_sem, fs_sem, fr_sem, seen,
):
    snaps, planes = u_buf.shape[0], u_buf.shape[1]
    cells, lanes = vel.shape[3], vel.shape[4]
    half = snaps // 2
    rows = half * cells
    edge = half * 3
    me = lax.axis_index("span")
    mw = lax.axis_index("wall")

    def ring(d):
        return lax.rem(me + span_count + d, span_count)

    down, up = ring(-1), ring(1)

    def load(i, src, dst):
        copy = pltpu.make_async_copy(src, dst, local_sem.at[i])
        copy.start()
        return copy

    mid = pl.ds(3, planes)
    load_pick = load(0, pick_hbm, pick_ref)
    load_u = load(1, vel.at[:, 0, mid], u_buf)
    load_v = load(2, vel.at[:, 1, mid], v_buf.at[:, mid])
    load_rest = [
        load(3, gather_hbm, gather_ref),
        load(4, vel.at[:, 2], w_buf),
        load(5, vel.at[:, 1, pl.ds(0, 3)], v_buf.at[:, pl.ds(0, 3)]),
        load(6, vel.at[:, 1, pl.ds(3 + planes, 3)], v_buf.at[:, pl.ds(3 + planes, 3)]),
        load(7, wall_hbm, wall_ref),
        load(8, scatter_hbm, scatter_ref),
        load(9, metric_hbm, metric_ref),
        load(10, inside_hbm, inside_ref),
        load(11, outside_hbm, outside_ref),
    ]

    barrier = pltpu.get_barrier_semaphore()
    for peer in (down, up):
        pl.semaphore_signal(barrier, inc=1, device_id=(peer, mw), device_id_type=MESH)
    for d in range(1, wall_count):
        pl.semaphore_signal(
            barrier, inc=1, device_id=(me, lax.rem(mw + d, wall_count)), device_id_type=MESH
        )

    def tell(phase):
        for peer in (ring(-(1 << phase)), ring(1 << phase)):
            pl.semaphore_signal(seen.at[phase], inc=1, device_id=(peer, mw), device_id_type=MESH)

    def hear(phase):
        pl.semaphore_wait(seen.at[phase], 2)

    def rows_of(value):
        return value.astype(F32).reshape(rows, lanes).astype(BF)

    def wide(buf, p):
        return jnp.concatenate(
            [rows_of(buf[k * half : (k + 1) * half, p]) for k in range(2)], axis=1
        )

    odd = lax.rem(me, 2)

    def piece(c, p, turn):
        side = 1 - odd if turn == 0 else odd
        here = pl.multiple_of(side * edge, edge)
        there = pl.multiple_of((1 - side) * edge, edge)
        return pltpu.make_async_remote_copy(
            send_buf.at[c, p, pl.ds(here, edge)], halo_buf.at[c, p, pl.ds(there, edge)],
            hs_sem.at[c, p, side], hr_sem.at[c, p, side],
            device_id=(ring(2 * side - 1), mw), device_id_type=MESH,
        )

    halo = []
    for c in range(2):
        if c == 0:
            load_pick.wait()
            load_u.wait()
        else:
            load_v.wait()
        for p in range(planes):
            f = wide(u_buf, p) if c == 0 else wide(v_buf, 3 + p)
            flat[c, p] = f
            send_buf[c, p] = dot(pick_ref[...], f).astype(BF)
            if c == 0 and p == 0:
                pl.semaphore_wait(barrier, 2 + wall_count - 1)
            halo.append([piece(c, p, turn) for turn in range(2)])
            halo[-1][0].start()
    for pair in halo:
        pair[1].start()

    phases = seen.shape[0]
    tell(0)
    for copy in load_rest:
        copy.wait()
    for p in range(planes):
        flat[2, p] = wide(w_buf, 3 + p)
    ysend_buf[...] = dot(
        jnp.concatenate([flat[2 * c, p] for c in range(2) for p in range(planes)], axis=1),
        gather_ref[...],
    ).astype(BF)

    y_up = pltpu.make_async_remote_copy(
        ysend_buf, ylo_buf, ys_sem.at[0], yr_sem.at[0],
        device_id=(me, lax.rem(mw + 1, wall_count)), device_id_type=MESH,
    )
    y_down = pltpu.make_async_remote_copy(
        ysend_buf, yhi_buf, ys_sem.at[1], yr_sem.at[1],
        device_id=(me, lax.rem(mw + wall_count - 1, wall_count)), device_id_type=MESH,
    )

    @pl.when(mw < wall_count - 1)
    def _():
        y_up.start()

    @pl.when(mw > 0)
    def _():
        y_down.start()

    @pl.when(mw == 0)
    def _():
        ylo_buf[...] = jnp.zeros_like(ylo_buf)

    @pl.when(mw == wall_count - 1)
    def _():
        yhi_buf[...] = jnp.zeros_like(yhi_buf)

    def along_x(k, carry):
        at = pl.ds(k * 4, 4)
        out = pl.ds(pl.multiple_of(k * 4 * cells, 4 * cells), 4 * cells)
        for c, buf in enumerate((v_buf, w_buf)):
            f = [buf[at, q].astype(F32) for q in range(6 + planes)]
            for p in range(planes):
                d = (
                    45.0 * (f[p + 4] - f[p + 2]) - 9.0 * (f[p + 5] - f[p + 1])
                    + (f[p + 6] - f[p])
                ).reshape(4 * cells, lanes)
                if c == 0:
                    acc[2, p, out] = d
                else:
                    acc[1, p, out] = -d
        return carry

    lax.fori_loop(0, snaps // 4, along_x, 0)

    if phases > 0:
        hear(0)
    if phases > 1:
        tell(1)

    @pl.when(mw > 0)
    def _():
        y_up.wait_recv()

    @pl.when(mw < wall_count - 1)
    def _():
        y_down.wait_recv()

    sides = jnp.concatenate([ylo_buf[...], yhi_buf[...]], axis=1)
    metric = metric_ref[...]
    for c in range(2):
        for p in range(planes):
            for k in range(2):
                g = (c * planes + p) * 2 + k
                at = slice(k * rows, (k + 1) * rows)
                f = flat[2 * c, p, :, k * lanes : (k + 1) * lanes]
                d = dot(f, wall_ref[...])
                d = d + dot(sides, scatter_ref[:, g * lanes : (g + 1) * lanes])
                d = d * metric
                if c == 0:
                    acc[2, p, at] = acc[2, p, at] - d
                else:
                    acc[0, p, at] = d

    def finish(comp, p, k, value):
        slab = comp * planes + p
        at = slice(k * rows, (k + 1) * rows)
        v = (value * (1.0 / 60.0)).astype(BF)
        vz[slab % 2, at] = v.astype(F32)

    def gram_of(slab):
        layers = [vz[slab % 2, pl.ds(z, snaps, stride=cells), :].astype(BF) for z in range(cells)]
        for z in range(cells):
            vort[z * snaps : (z + 1) * snaps, slab * lanes : (slab + 1) * lanes] = layers[z]
        a = jnp.concatenate(layers, axis=1)
        return lax.dot_general(
            a, jnp.concatenate([a, a], axis=0), (((1,), (1,)), ((), ())),
            preferred_element_type=F32,
        )

    for p in range(planes):
        for c in range(2):
            d = dot(inside_ref[...], flat[c, p])
            for k in range(2):
                at = slice(k * rows, (k + 1) * rows)
                part = d[:, k * lanes : (k + 1) * lanes]
                if c == 0:
                    acc[1, p, at] = acc[1, p, at] + part
                else:
                    acc[0, p, at] = acc[0, p, at] - part
    g = None
    for p in range(planes):
        for k in range(2):
            finish(2, p, k, acc[2, p, k * rows : (k + 1) * rows])
        part = gram_of(2 * planes + p)
        g = part if g is None else g + part
    if phases > 1:
        hear(1)
    for phase in range(2, phases):
        tell(phase)
        if phase < phases - 1:
            hear(phase)

    for c in range(2):
        for p in range(planes):
            for copy in halo[c * planes + p]:
                copy.wait_recv()
            d = dot(outside_ref[...], halo_buf[c, p])
            for k in range(2):
                at = slice(k * rows, (k + 1) * rows)
                part = d[:, k * lanes : (k + 1) * lanes]
                if c == 0:
                    finish(1, p, k, acc[1, p, at] + part)
                else:
                    finish(0, p, k, acc[0, p, at] - part)
            g = g + gram_of((1 - c) * planes + p)
    if phases > 2:
        hear(phases - 1)

    quarter = half // 2
    lane = lax.broadcasted_iota(jnp.int32, (8, 2 * snaps), 1)
    sub = lax.broadcasted_iota(jnp.int32, (8, 2 * snaps), 0)
    left = lane < snaps
    for i in range(quarter // 8):
        at = slice(8 * i, 8 * i + 8)
        piece_buf[mw, at] = jnp.where(left, g[at], g[quarter + 8 * i : quarter + 8 * i + 8])
    corner = None
    for i in range(4):
        part = g[half + 8 * i : half + 8 * i + 8]
        if i % 2 == 0:
            part = pltpu.roll(part, half, 1)
        corner = part if corner is None else jnp.where(lane < half * i, corner, part)
    piece_buf[mw, quarter : quarter + 8] = corner
    copies = []

    def remote(src, dst, send, recv, device):
        copy = pltpu.make_async_remote_copy(
            src, dst, send, recv, device_id=device, device_id_type=MESH
        )
        copy.start()
        return copy

    started = []
    for d in range(1, wall_count):
        w = lax.rem(mw + d, wall_count)
        started.append(
            remote(piece_buf.at[mw], piece_buf.at[mw], ps_sem.at[d], pr_sem.at[d], (me, w))
        )
    for copy in started:
        copy.wait_recv()
    copies += started
    total = piece_buf[0]
    for w in range(1, wall_count):
        total = total + piece_buf[w]
    low = 8 // wall_count
    corner_buf[...] = total[quarter : quarter + 8]
    sum_buf[me, 0:quarter] = total[:quarter]
    sum_buf[me, quarter : quarter + low] = corner_buf[pl.ds(mw * low, low)]
    others = [i + (me <= i).astype(jnp.int32) for i in range(span_count - 1)]
    parts = (pl.ds(0, quarter + low),)

    def to(turn, peer):
        mine = sum_buf.at[me, parts[turn]]
        copies.append(
            remote(mine, mine, ss_sem.at[turn, peer], sr_sem.at[turn, me], (peer, mw))
        )

    def arrived(turn):
        for peer in others:
            theirs = sum_buf.at[peer, parts[turn]]
            pltpu.make_async_remote_copy(
                theirs, theirs, ss_sem.at[turn, peer], sr_sem.at[turn, peer],
                device_id=(peer, mw), device_id_type=MESH,
            ).wait_recv()

    for peer in others:
        to(0, peer)
    arrived(0)
    total = sum_buf[0]
    for i in range(1, span_count):
        total = total + sum_buf[i]
    total = total / total_rows
    full_buf[mw] = total[quarter:]
    started = []
    for d in range(1, wall_count):
        w = lax.rem(mw + d, wall_count)
        started.append(
            remote(full_buf.at[mw], full_buf.at[mw], fs_sem.at[d], fr_sem.at[d], (me, w))
        )
    total = total[:quarter]
    top = jnp.concatenate([total, pltpu.roll(total, snaps, 1)], axis=0)
    turned = jnp.concatenate([top] * 4, axis=0).T
    groups = []
    for i in range(snaps // 8):
        if 8 * i < half:
            value = top[8 * i : 8 * i + 8]
        else:
            value = jnp.where(lane < half, turned[8 * i : 8 * i + 8], 0.0)
        groups.append(jnp.where(left, value, (lane - snaps - 8 * i == sub).astype(F32)))
    first = half // 8
    for b, (p, s) in enumerate(eliminate(groups, 0, first)):
        state_ref[8 * b : 8 * b + 8] = scaled_rows(p, s)
    for copy in started:
        copy.wait_recv()
    copies += started
    for w in range(wall_count):
        corner_buf[w * low : (w + 1) * low] = full_buf[w]
    total = corner_buf[...]
    inner = jnp.logical_and(lane >= half, left)
    for i in range(first):
        part = total if i == 1 else pltpu.roll(total, (5 - i) % 4 * half, 1)
        b = first + i
        state_ref[8 * b : 8 * b + 8] = groups[b] + jnp.where(inner, part, 0.0)

    for copy in copies:
        copy.wait_send()
    for pair in halo:
        for copy in pair:
            copy.wait_send()

    @pl.when(mw < wall_count - 1)
    def _():
        y_up.wait_send()

    @pl.when(mw > 0)
    def _():
        y_down.wait_send()


def modes_kernel(vort, state_ref, out_hbm, r_hbm, out, r_ref, sem):
    snaps, comps, planes, cells, lanes = out.shape
    half = snaps // 2
    first = half // 8
    groups = [state_ref[8 * i : 8 * i + 8] for i in range(snaps // 8)]

    def blocks():
        for b in range(first):
            row = groups[b]
            yield [jnp.broadcast_to(row[k : k + 1], (8, 2 * snaps)) for k in range(8)], row
        for p, s in eliminate(groups, first, 2 * first):
            q = [p[k] / jnp.sqrt(s[k]) for k in range(8)]
            row = q[0]
            for k in range(1, 8):
                row = jnp.where(sub8 == k, q[k], row)
            yield q, row

    lane8 = lax.broadcasted_iota(jnp.int32, (8, 2 * snaps), 1)
    sub8 = lax.broadcasted_iota(jnp.int32, (8, 2 * snaps), 0)
    cuts = [first, first + first // 2, 2 * first]
    layer = lane8 // snaps
    scaled = []
    stores = []
    for b, (q, row) in enumerate(blocks()):
        row = jnp.where(lane8 < sub8 + 8 * b, 0.0, row)
        r_ref[8 * b : 8 * b + 8] = row[:, :snaps]
        for value in q:
            twice = jnp.where(lane8 < snaps, pltpu.roll(value, snaps, 1), value)
            scaled.append(
                jnp.concatenate(
                    [jnp.where(layer + 2 * v == sub8, twice, 0.0) for v in range(cells // 2)],
                    axis=1,
                )
            )
        if b + 1 in cuts:
            w = jnp.concatenate(scaled, axis=0).astype(BF)
            scaled = []
            n = cuts.index(b + 1)
            start, stop = (8 * cuts[n - 1] if n else 0), 8 * (b + 1)
            block = stop - start
            m = dot(w, vort[...])
            at = pl.ds(start, block)
            for comp in range(comps):
                for p_ in range(planes):
                    slab = comp * planes + p_
                    out[start:stop, comp, p_] = (
                        m[:, slab * lanes : (slab + 1) * lanes]
                        .reshape(block, cells, lanes).astype(BF)
                    )
            store = pltpu.make_async_copy(out.at[at], out_hbm.at[at], sem.at[n])
            store.start()
            stores.append(store)
    store = pltpu.make_async_copy(r_ref, r_hbm, sem.at[4])
    store.start()
    stores.append(store)
    for store in stores:
        store.wait()


def per_device(velocity, wall_metric):
    snaps, comps, depth, cells, lanes = velocity.shape
    planes = depth - 6
    spans, walls = lax.axis_size("span"), lax.axis_size("wall")
    phases, reach = 0, 1
    while 2 * reach < spans:
        phases, reach = phases + 1, 2 * reach
    total_rows = 3 * planes * cells * spans * lanes * walls
    consts = constants(snaps, cells, lanes, planes)
    vmem = pl.BlockSpec(memory_space=pltpu.VMEM)
    hbm = pl.BlockSpec(memory_space=pl.ANY)
    dma = pltpu.SemaphoreType.DMA
    half = snaps // 2
    wide = snaps * cells
    rows = half * cells
    edge = half * 3
    slabs = comps * planes
    vorticity, state = pl.pallas_call(
        functools.partial(kernel, spans, walls, total_rows),
        out_shape=(
            pltpu.VMEM((wide, slabs * lanes), BF),
            pltpu.VMEM((snaps, 2 * snaps), F32),
        ),
        in_specs=[hbm] * (2 + len(consts)),
        out_specs=(vmem, vmem),
        scratch_shapes=[
            pltpu.VMEM((1, lanes), F32),
            *[pltpu.VMEM(a.shape, a.dtype) for a in consts],
            pltpu.VMEM((snaps, planes, cells, lanes), BF),
            pltpu.VMEM((snaps, depth, cells, lanes), BF),
            pltpu.VMEM((snaps, depth, cells, lanes), BF),
            pltpu.VMEM((3, planes, rows, 2 * lanes), BF),
            pltpu.VMEM((2, planes, 2 * edge, 2 * lanes), BF),
            pltpu.VMEM((2, planes, 2 * edge, 2 * lanes), BF),
            pltpu.VMEM((rows, lanes), BF),
            pltpu.VMEM((rows, lanes), BF),
            pltpu.VMEM((rows, lanes), BF),
            pltpu.VMEM((3, planes, wide, lanes), F32),
            pltpu.VMEM((2, wide, lanes), F32),
            pltpu.VMEM((walls, half // 2 + 8, 2 * snaps), F32),
            pltpu.VMEM((spans, half // 2 + 8 // walls, 2 * snaps), F32),
            pltpu.VMEM((8, 2 * snaps), F32),
            pltpu.VMEM((walls, 8 // walls, 2 * snaps), F32),
            dma((12,)),
            dma((2, planes, 2)),
            dma((2, planes, 2)),
            dma((2,)),
            dma((2,)),
            dma((walls,)),
            dma((walls,)),
            dma((1, spans)),
            dma((1, spans)),
            dma((walls,)),
            dma((walls,)),
            pltpu.SemaphoreType.REGULAR((phases,)),
        ],
        compiler_params=pltpu.CompilerParams(
            collective_id=0, has_side_effects=True, vmem_limit_bytes=60 << 20
        ),
        name="pod",
    )(velocity, wall_metric.reshape(1, lanes), *consts)
    return pl.pallas_call(
        modes_kernel,
        out_shape=(
            jax.ShapeDtypeStruct((snaps, comps, planes, cells, lanes), BF),
            jax.ShapeDtypeStruct((snaps, snaps), F32),
        ),
        in_specs=[vmem, vmem],
        out_specs=(hbm, hbm),
        scratch_shapes=[
            pltpu.VMEM((snaps, comps, planes, cells, lanes), BF),
            pltpu.VMEM((snaps, snaps), F32),
            dma((5,)),
        ],
        compiler_params=pltpu.CompilerParams(vmem_limit_bytes=32 << 20),
        name="modes",
    )(vorticity, state)


def solution(mesh):
    in_specs = (P(None, None, None, "span", "wall"), P("wall"))
    out_specs = (P(None, None, None, "span", "wall"), P())
    return jax.shard_map(
        per_device, mesh=mesh, in_specs=in_specs, out_specs=out_specs, check_vma=False
    )
```
